32 devices in a mesh: dev: 32 (over z, y, x, core).
Axes of the slice: x: 2, y: 2, z: 4, core: 2. Of those that a mesh axis runs over, the one named last changes fastest.
Arguments:
- layer_input: bfloat16 [5120, 1024], P('dev'), may hold values from -6 to 6
- ln1_gain: bfloat16 [1024], P('dev'), may hold values from 0.5 to 1.5
- ln1_bias: bfloat16 [1024], P('dev'), may hold values from -3 to 3
- qkv_weight: bfloat16 [1024, 3072], P('dev'), may hold values from -1.40625 to 1.40625
- qkv_bias: bfloat16 [3072], P('dev'), may hold values from -3 to 3
- dense_weight: bfloat16 [1024, 1024], P('dev'), may hold values from -0.75 to 0.75
- dense_bias: bfloat16 [1024], P('dev'), may hold values from -3 to 3
- ln2_gain: bfloat16 [1024], P('dev'), may hold values from 0.5 to 1.5
- ln2_bias: bfloat16 [1024], P('dev'), may hold values from -3 to 3
- fc_in_weight: bfloat16 [1024, 4096], P('dev'), may hold values from -0.1875 to 0.1875
- fc_in_bias: bfloat16 [4096], P('dev'), may hold values from -3 to 3
- fc_out_weight: bfloat16 [4096, 1024], P('dev'), may hold values from -0.09375 to 0.09375
- fc_out_bias: bfloat16 [1024], P('dev'), may hold values from -3 to 3
- positions: int32 [5120], P('dev'), may hold values from 0 to 511, as said below
- cotangent: bfloat16 [5120, 1024], P('dev'), may hold values from -6 to 6
Outputs:
- output: bfloat16 [5120, 1024], P('dev')
- grad_input: float32 [5120, 1024], P('dev')
- grad_ln1_gain: float32 [1024], P('dev')
- grad_ln1_bias: float32 [1024], P('dev')
- grad_qkv_weight: float32 [1024, 3072], P('dev')
- grad_qkv_bias: float32 [3072], P('dev')
- grad_dense_weight: float32 [1024, 1024], P('dev')
- grad_dense_bias: float32 [1024], P('dev')
- grad_ln2_gain: float32 [1024], P('dev')
- grad_ln2_bias: float32 [1024], P('dev')
- grad_fc_in_weight: float32 [1024, 4096], P('dev')
- grad_fc_in_bias: float32 [4096], P('dev')
- grad_fc_out_weight: float32 [4096, 1024], P('dev')
- grad_fc_out_bias: float32 [1024], P('dev')
The draws below stay inside these ranges and needn't reach their ends.
Inputs may be any that keep to these rules, and one draw needn't show every extreme that they name: `positions`: documents lie end to end over all tokens; a token of position p has the p tokens before it in its document, and a token of position 0 starts a document; no document is longer than 512 tokens, and in every draw one document has exactly 512 tokens.
All inputs are finite; a program needn't handle non-finite values.
Results may differ from the reference program's by a relative error of at most 0.0095.
Values may be sent and summed in bfloat16 or wider, within the bound.
A program may use at most 256 MiB of HBM per device.

```python
import jax
import jax.numpy as jnp
from jax import lax

D = 1024
HEADS = 16
HD = 64
ROT = 16
FF = 4096
SEQ = 512
TOKENS = 5120


def draw_positions(key, part):
    own_key = jax.random.fold_in(key, 11)
    token_index = jnp.arange(TOKENS, dtype=jnp.int32)
    column = token_index % SEQ
    first_key, second_key = jax.random.split(own_key)
    coin_marks = jax.random.randint(first_key, (TOKENS,), 0, max(SEQ // 4, 2))
    offset = jax.random.randint(second_key, (), SEQ // 4, 3 * SEQ // 4 + 1)
    long_start = TOKENS // 2 - offset
    inside = (token_index > long_start) & (token_index < long_start + SEQ)
    starts = ((column == 0) | (coin_marks == 0) | (token_index == long_start) | (token_index == long_start + SEQ)) & jnp.logical_not(inside)
    doc_begin = lax.cummax(jnp.where(starts, token_index, 0), axis=0)
    return (token_index - doc_begin).astype(jnp.int32)


def draw_qkv_weight(key, part):
    own_key = jax.random.fold_in(key, 3)
    std_scale = D ** (-0.5)
    base_draw = jnp.clip(jax.random.normal(own_key, (D, 3 * D), jnp.float32), -6.0, 6.0)
    return (base_draw * std_scale).astype(jnp.bfloat16)


def raised(values, rng, source, target, shards_of, factor):
    owner, partner = [(jnp.arange(values.shape[axis_at]) // (values.shape[axis_at] // shards_of)).reshape([-1 if axis == axis_at else 1 for axis in range(values.ndim)]) for axis_at in (source, target)]
    chosen = jax.random.permutation(rng, shards_of)[partner]
    strong = (owner == chosen) | (owner == (partner + shards_of // 2) % shards_of)
    return jnp.where(strong, factor * values, values)


def shard_levels(rng, shape, shards, least, top_value):
    def one(dim, parts):
        heights = jax.random.uniform(jax.random.fold_in(jax.random.fold_in(rng, 6), dim), (parts,), jnp.float32, least / len(shards), top_value / len(shards))
        return jnp.repeat(jnp.exp(heights), shape[dim] // parts).reshape((-1,) + (1,) * (len(shape) - dim - 1))

    level = one(*shards[0])
    for cut in shards[1:]:
        level = level * one(*cut)
    return level


def noise(key, dims, scale, most, cuts=(), kind=jnp.bfloat16):
    values = scale * jax.random.normal(key, dims, jnp.float32)
    if cuts:
        values = values * shard_levels(key, dims, cuts, -0.22, 0.18)
    return jnp.clip(values, -most, most).astype(kind)


def gaussian_with(key, shape, scale, limit, cuts, heavy, held_as=jnp.bfloat16):
    entries = scale * jax.random.normal(key, shape, jnp.float32)
    if cuts:
        entries = entries * shard_levels(key, shape, cuts, -0.22, 0.18)
    return jnp.clip(raised(entries, jax.random.fold_in(key, 3), *heavy), -limit, limit).astype(held_as)


def setup_inputs(seed: int = 0) -> dict:
    key_of = jax.random.split(jax.random.key(seed), 16)
    layer_input = gaussian_with(key_of[0], (TOKENS, D), 1.0, 6.0, ((0, 32),), (0, 1, 32, 2.75))
    ln1_gain = jnp.clip(1.0 + 0.1 * jax.random.normal(key_of[1], (D,), jnp.float32), 0.5, 1.5).astype(jnp.bfloat16)
    ln1_bias = noise(key_of[2], (D,), 0.5, 3.0, ((0, 32),))
    qkv_weight = draw_qkv_weight(jax.random.fold_in(key_of[15], 71), 0)
    qkv_bias = noise(key_of[4], (3 * D,), 0.5, 3.0, ((0, 32),))
    dense_weight = noise(key_of[5], (D, D), (D // 16) ** -0.5, 0.75, ((0, 32),))
    dense_bias = noise(key_of[6], (D,), 0.5, 3.0, ((0, 32),))
    ln2_gain = jnp.clip(1.0 + 0.1 * jax.random.normal(key_of[7], (D,), jnp.float32), 0.5, 1.5).astype(jnp.bfloat16)
    ln2_bias = noise(key_of[8], (D,), 0.5, 3.0, ((0, 32),))
    fc_in_weight = noise(key_of[9], (D, FF), D ** -0.5, 0.1875, ((0, 32),))
    fc_in_bias = noise(key_of[10], (FF,), 0.5, 3.0, ((0, 32),))
    fc_out_weight = noise(key_of[11], (FF, D), FF ** -0.5, 0.09375, ((0, 32),))
    fc_out_bias = noise(key_of[12], (D,), 0.5, 3.0, ((0, 32),))
    positions = draw_positions(jax.random.fold_in(key_of[15], 71), 0)
    cotangent = gaussian_with(key_of[14], (TOKENS, D), 1.0, 6.0, ((0, 32),), (0, 1, 32, 2.75))
    return dict(layer_input=layer_input, ln1_gain=ln1_gain, ln1_bias=ln1_bias, qkv_weight=qkv_weight, qkv_bias=qkv_bias, dense_weight=dense_weight, dense_bias=dense_bias, ln2_gain=ln2_gain, ln2_bias=ln2_bias, fc_in_weight=fc_in_weight, fc_in_bias=fc_in_bias, fc_out_weight=fc_out_weight, fc_out_bias=fc_out_bias, positions=positions, cotangent=cotangent)


EPSILON = 1e-05
ROPE_BASE = 10000.0

def norm_stats(inputs):
    values_f = inputs.astype(jnp.float32)
    centre = lax.optimization_barrier(jnp.mean(values_f, axis=-1, keepdims=True))
    shifted = values_f - centre
    variance = lax.optimization_barrier(jnp.mean(shifted * shifted, axis=-1, keepdims=True))
    inv_scale = lax.rsqrt(variance + EPSILON)
    return (shifted * inv_scale, inv_scale)

def rotary_tables(positions, rot_half):
    counter = jnp.arange(rot_half).astype(jnp.float32)
    frequency = ROPE_BASE ** (-2.0 * counter / (2.0 * rot_half))
    angles = positions.astype(jnp.float32)[:, None] * frequency[None, :]
    return (jnp.cos(angles), jnp.sin(angles))

def rotate(head_rows, cos_table, sin_table, orient):
    halfway = cos_table.shape[-1]
    leading = head_rows[..., :halfway]
    trailing = head_rows[..., halfway:2 * halfway]
    remainder = head_rows[..., 2 * halfway:]
    cosine = cos_table[:, None, :]
    sine_part = orient * sin_table[:, None, :]
    return jnp.concatenate([leading * cosine - trailing * sine_part, trailing * cosine + leading * sine_part, remainder], axis=-1)

def gelu_pair(pre_act):
    cumulative = 0.5 * (1.0 + lax.erf(pre_act * 0.7071067811865476))
    density = jnp.exp(-0.5 * pre_act * pre_act) * 0.3989422804014327
    return (pre_act * cumulative, cumulative + pre_act * density)

def row_sum_product(left_side, right_side):
    return lax.dot_general(left_side, right_side, (((0,), (0,)), ((), ())), preferred_element_type=jnp.float32)

def times_transpose(left_side, right_side):
    return lax.dot_general(left_side, right_side, (((1,), (1,)), ((), ())), preferred_element_type=jnp.float32)

def masked_scores(queries, keys_rot, allowed):
    scores = jnp.einsum('qhd,khd->hqk', queries.astype(jnp.float32), keys_rot.astype(jnp.float32)) * HD ** (-0.5)
    return jnp.where(allowed[None], scores, -jnp.inf)

def attend(queries, keys_rot, values_v, allowed):
    scores = masked_scores(queries, keys_rot, allowed)
    row_max = lax.optimization_barrier(jnp.max(scores, axis=-1, keepdims=True))
    exp_total = lax.optimization_barrier(jnp.sum(jnp.exp(scores - row_max), axis=-1, keepdims=True))
    log_total = row_max + jnp.log(exp_total)
    probs_b = jnp.exp(scores - log_total).astype(jnp.bfloat16)
    context = jnp.einsum('hqk,khd->qhd', probs_b.astype(jnp.float32), values_v.astype(jnp.float32))
    return (context, log_total)

def attend_back(queries, keys_rot, values_v, allowed, log_total, grad_context):
    scores = masked_scores(queries, keys_rot, allowed)
    probs = jnp.exp(scores - log_total)
    probs_b = probs.astype(jnp.bfloat16)
    grad_probs = jnp.einsum('qhd,khd->hqk', grad_context.astype(jnp.float32), values_v.astype(jnp.float32))
    row_dot = lax.optimization_barrier(jnp.sum(probs * grad_probs, axis=-1, keepdims=True))
    grad_scores = (probs * (grad_probs - row_dot) * HD ** (-0.5)).astype(jnp.bfloat16)
    grad_queries = jnp.einsum('hqk,khd->qhd', grad_scores.astype(jnp.float32), keys_rot.astype(jnp.float32))
    grad_keys = jnp.einsum('hqk,qhd->khd', grad_scores.astype(jnp.float32), queries.astype(jnp.float32))
    grad_values = jnp.einsum('hqk,qhd->khd', probs_b.astype(jnp.float32), grad_context.astype(jnp.float32))
    return (grad_queries, grad_keys, grad_values)

def reference(layer_input, ln1_gain, ln1_bias, qkv_weight, qkv_bias, dense_weight, dense_bias, ln2_gain, ln2_bias, fc_in_weight, fc_in_bias, fc_out_weight, fc_out_bias, positions, cotangent):
    num_seqs = layer_input.shape[0] // SEQ
    gain_one = ln1_gain.astype(jnp.float32)
    shift_one = ln1_bias.astype(jnp.float32)
    gain_two = ln2_gain.astype(jnp.float32)
    shift_two = ln2_bias.astype(jnp.float32)
    bias_qkv = qkv_bias.astype(jnp.float32)
    bias_dense = dense_bias.astype(jnp.float32)
    bias_in = fc_in_bias.astype(jnp.float32)
    bias_out = fc_out_bias.astype(jnp.float32)
    input_blocks = layer_input.reshape(num_seqs, SEQ, D)
    place_blocks = positions.reshape(num_seqs, SEQ)
    top_blocks = cotangent.reshape(num_seqs, SEQ, D)

    def project(item):
        tokens_in, place = item
        normed, inv_scale = norm_stats(tokens_in)
        left_attn = (normed * gain_one + shift_one).astype(jnp.bfloat16)
        mixed_qkv = jnp.dot(left_attn, qkv_weight, preferred_element_type=jnp.float32) + bias_qkv
        cos_table, sin_table = rotary_tables(place, ROT // 2)
        queries = rotate(mixed_qkv[:, :D].reshape(SEQ, HEADS, HD), cos_table, sin_table, 1.0).astype(jnp.bfloat16)
        keys_rot = rotate(mixed_qkv[:, D:2 * D].reshape(SEQ, HEADS, HD), cos_table, sin_table, 1.0).astype(jnp.bfloat16)
        values_v = mixed_qkv[:, 2 * D:].reshape(SEQ, HEADS, HD).astype(jnp.bfloat16)
        return (queries, keys_rot, values_v)
    all_queries, all_keys, all_values = lax.map(project, (input_blocks, place_blocks))
    empty_block = jnp.zeros((1, SEQ, HEADS, HD), jnp.bfloat16)
    prev_keys = jnp.concatenate([empty_block, all_keys[:-1]], axis=0)
    prev_values = jnp.concatenate([empty_block, all_values[:-1]], axis=0)

    def attention_block(item):
        queries, keys_before, keys_now, values_before, values_now, place, grad_top = item
        win_keys = jnp.concatenate([keys_before, keys_now], axis=0)
        win_values = jnp.concatenate([values_before, values_now], axis=0)
        query_index = jnp.arange(SEQ, dtype=jnp.int32) + SEQ
        key_index = jnp.arange(2 * SEQ, dtype=jnp.int32)
        spread = query_index[:, None] - key_index[None, :]
        allowed = (spread >= 0) & (spread <= place[:, None])
        context, log_total = attend(queries, win_keys, win_values, allowed)
        context_b = context.reshape(SEQ, D).astype(jnp.bfloat16)
        grad_context = times_transpose(grad_top, dense_weight).astype(jnp.bfloat16).reshape(SEQ, HEADS, HD)
        g_queries, g_keys, g_values = attend_back(queries, win_keys, win_values, allowed, log_total, grad_context)
        return (context_b, g_queries, g_keys, g_values)
    all_context, all_gq, win_gk, win_gv = lax.map(attention_block, (all_queries, prev_keys, all_keys, prev_values, all_values, place_blocks, top_blocks))
    empty_grad = jnp.zeros((1, SEQ, HEADS, HD), jnp.float32)
    own_gk = win_gk[:, SEQ:] + jnp.concatenate([win_gk[1:, :SEQ], empty_grad], axis=0)
    own_gv = win_gv[:, SEQ:] + jnp.concatenate([win_gv[1:, :SEQ], empty_grad], axis=0)

    def one_block(totals, seq_item):
        tokens_in, place, grad_top, context_b, g_queries, g_keys, g_values = seq_item
        normed, inv_scale = norm_stats(tokens_in)
        left_attn = (normed * gain_one + shift_one).astype(jnp.bfloat16)
        left_mlp = (normed * gain_two + shift_two).astype(jnp.bfloat16)
        cos_table, sin_table = rotary_tables(place, ROT // 2)
        attn_out = jnp.dot(context_b, dense_weight, preferred_element_type=jnp.float32) + bias_dense
        pre_act = jnp.dot(left_mlp, fc_in_weight, preferred_element_type=jnp.float32) + bias_in
        activated, gelu_slope = gelu_pair(pre_act)
        activated_b = activated.astype(jnp.bfloat16)
        mlp_out = jnp.dot(activated_b, fc_out_weight, preferred_element_type=jnp.float32) + bias_out
        result = (tokens_in.astype(jnp.float32) + attn_out + mlp_out).astype(jnp.bfloat16)
        top_f = grad_top.astype(jnp.float32)
        g_dense_w = row_sum_product(context_b, grad_top)
        g_dense_b = lax.optimization_barrier(jnp.sum(top_f, axis=0))
        g_out_w = row_sum_product(activated_b, grad_top)
        g_out_b = lax.optimization_barrier(jnp.sum(top_f, axis=0))
        grad_pre = times_transpose(grad_top, fc_out_weight) * gelu_slope
        grad_pre_b = grad_pre.astype(jnp.bfloat16)
        g_in_w = row_sum_product(left_mlp, grad_pre_b)
        g_in_b = lax.optimization_barrier(jnp.sum(grad_pre, axis=0))
        grad_left_mlp = times_transpose(grad_pre_b, fc_in_weight)
        back_queries = rotate(g_queries, cos_table, sin_table, -1.0)
        back_keys = rotate(g_keys, cos_table, sin_table, -1.0)
        grad_qkv = jnp.concatenate([back_queries.reshape(SEQ, D), back_keys.reshape(SEQ, D), g_values.reshape(SEQ, D)], axis=1)
        grad_qkv_b = grad_qkv.astype(jnp.bfloat16)
        g_qkv_w = row_sum_product(left_attn, grad_qkv_b)
        g_qkv_b = lax.optimization_barrier(jnp.sum(grad_qkv, axis=0))
        grad_left_attn = times_transpose(grad_qkv_b, qkv_weight)
        g_gain_one = lax.optimization_barrier(jnp.sum(grad_left_attn * normed, axis=0))
        g_shift_one = lax.optimization_barrier(jnp.sum(grad_left_attn, axis=0))
        g_gain_two = lax.optimization_barrier(jnp.sum(grad_left_mlp * normed, axis=0))
        g_shift_two = lax.optimization_barrier(jnp.sum(grad_left_mlp, axis=0))
        grad_normed = grad_left_attn * gain_one + grad_left_mlp * gain_two
        grad_in = top_f + inv_scale * (grad_normed - lax.optimization_barrier(jnp.mean(grad_normed, axis=-1, keepdims=True)) - normed * lax.optimization_barrier(jnp.mean(grad_normed * normed, axis=-1, keepdims=True)))
        terms = (g_gain_one, g_shift_one, g_qkv_w, g_qkv_b, g_dense_w, g_dense_b, g_gain_two, g_shift_two, g_in_w, g_in_b, g_out_w, g_out_b)
        totals = jax.tree.map(jnp.add, totals, terms)
        return (totals, (result, grad_in))
    zero_totals = (jnp.zeros((D,), jnp.float32), jnp.zeros((D,), jnp.float32), jnp.zeros((D, 3 * D), jnp.float32), jnp.zeros((3 * D,), jnp.float32), jnp.zeros((D, D), jnp.float32), jnp.zeros((D,), jnp.float32), jnp.zeros((D,), jnp.float32), jnp.zeros((D,), jnp.float32), jnp.zeros((D, FF), jnp.float32), jnp.zeros((FF,), jnp.float32), jnp.zeros((FF, D), jnp.float32), jnp.zeros((D,), jnp.float32))
    seq_items = (input_blocks, place_blocks, top_blocks, all_context, all_gq, own_gk, own_gv)
    totals, stacked = lax.scan(one_block, zero_totals, seq_items)
    outputs = stacked[0].reshape(num_seqs * SEQ, D)
    grad_in = stacked[1].reshape(num_seqs * SEQ, D)
    return (outputs, grad_in, totals[0], totals[1], totals[2], totals[3], totals[4], totals[5], totals[6], totals[7], totals[8], totals[9], totals[10], totals[11])
```

```python
import functools

import jax
import jax.numpy as jnp
from jax import lax
from jax.experimental import pallas as pl
from jax.experimental.pallas import tpu as pltpu
from jax.sharding import Mesh
from jax.sharding import PartitionSpec as P

HEADS = 16
HD = 64
ROT = 16
REACH = 512
GROUP = 8
BLOCK = 256
EPSILON = 1e-05
ROPE_BASE = 10000.0
MESH = pl.DeviceIdType.MESH
BF = jnp.bfloat16
F32 = jnp.float32
VMEM_LIMIT = 58 * 2**20


def norm_stats(inputs):
    values_f = inputs.astype(jnp.float32)
    centre = jnp.mean(values_f, axis=-1, keepdims=True)
    shifted = values_f - centre
    variance = jnp.mean(shifted * shifted, axis=-1, keepdims=True)
    inv_scale = lax.rsqrt(variance + EPSILON)
    return (shifted * inv_scale, inv_scale)


def rotary_tables(positions, lanes):
    place = jnp.arange(lanes, dtype=jnp.int32) % HD
    counter = (place % (ROT // 2)).astype(jnp.float32)
    frequency = ROPE_BASE ** (-2.0 * counter / ROT)
    frequency = jnp.where(place < ROT, frequency, 0.0)
    angles = positions.astype(jnp.float32)[:, None] * frequency[None, :]
    sine = jnp.sin(angles)
    lower = jnp.where(place < ROT // 2, -sine, 0.0)
    upper = jnp.where(place >= ROT // 2, sine, 0.0)
    return (jnp.cos(angles), lower, upper)


def rotate(rows, tables, orient):
    cosine, lower, upper = tables
    ahead = jnp.roll(rows, -(ROT // 2), axis=1)
    behind = jnp.roll(rows, ROT // 2, axis=1)
    return rows * cosine + orient * (ahead * lower + behind * upper)


def gelu_pair(pre_act):
    cumulative = 0.5 * (1.0 + lax.erf(pre_act * 0.7071067811865476))
    density = jnp.exp(-0.5 * pre_act * pre_act) * 0.3989422804014327
    return (pre_act * cumulative, cumulative + pre_act * density)


def row_sum_product(left_side, right_side):
    return lax.dot_general(
        left_side, right_side, (((0,), (0,)), ((), ())), preferred_element_type=jnp.float32
    )


def times_transpose(left_side, right_side):
    return lax.dot_general(
        left_side, right_side, (((1,), (1,)), ((), ())), preferred_element_type=jnp.float32
    )


def remote(src, dst, send, recv, g, r):
    return pltpu.make_async_remote_copy(
        src_ref=src, dst_ref=dst, send_sem=send, recv_sem=recv,
        device_id=(g, r), device_id_type=MESH,
    )


def enter(outer, inner):
    g, r = lax.axis_index("g"), lax.axis_index("r")
    bar = pltpu.get_barrier_semaphore()
    for j in range(1, inner):
        pl.semaphore_signal(bar, inc=1, device_id=(g, r ^ j), device_id_type=MESH)
    for k in range(1, outer):
        pl.semaphore_signal(
            bar, inc=1, device_id=(lax.rem(g + k, outer), r), device_id_type=MESH
        )
    pl.semaphore_wait(bar, inner + outer - 2)
    return g, r


class PlaneSwap:
    def __init__(self, inner, g, r, src, dst, send, recv):
        self.copies = [
            remote(src(r ^ j), dst(r), send.at[j], recv.at[j], g, r ^ j) for j in range(1, inner)
        ]
        self.landed = [
            remote(dst(r ^ j), dst(r ^ j), send.at[j], recv.at[j], g, r ^ j)
            for j in range(1, inner)
        ]

    def start(self):
        for copy in self.copies:
            copy.start()

    def arrive(self):
        for copy in self.landed:
            copy.wait_recv()

    def sent(self):
        for copy in self.copies:
            copy.wait_send()


def near(outer, g, other):
    if outer != 4:
        return g != other
    return (g != other) & (jnp.abs(g - other) <= 2)


class ColumnGather:
    def __init__(self, outer, g, r, own, full, send, recv):
        self.outer, self.g, self.r = outer, g, r
        self.own, self.full, self.send, self.recv = own, full, send, recv

    def copy(self, dst):
        return remote(
            self.own, self.full.at[self.g], self.send.at[dst], self.recv.at[self.g], dst, self.r
        )

    def onward(self, src, dst):
        return remote(
            self.full.at[src], self.full.at[src], self.send.at[self.outer],
            self.recv.at[src], dst, self.r,
        )

    def start(self):
        order = range(self.outer)
        for dst in order:
            @pl.when(near(self.outer, self.g, dst))
            def _(dst=dst):
                self.copy(dst).start()

    def forward(self):
        if self.outer != 4:
            return
        for via, src, dst in ((2, 0, 3), (1, 3, 0)):
            @pl.when(self.g == via)
            def _(src=src, dst=dst):
                self.onward(src, dst).wait_recv()
                self.onward(src, dst).start()

    def arrive(self):
        for src in range(self.outer):
            waits = self.g != src
            if self.outer == 4 and src in (0, 3):
                waits = waits & (self.g != (2 if src == 0 else 1))
            @pl.when(waits)
            def _(src=src):
                self.onward(src, src).wait_recv()

    def sent(self):
        for dst in range(self.outer):
            @pl.when(near(self.outer, self.g, dst))
            def _(dst=dst):
                self.copy(dst).wait_send()
        if self.outer == 4:
            for via, src, dst in ((2, 0, 3), (1, 3, 0)):
                @pl.when(self.g == via)
                def _(src=src, dst=dst):
                    self.onward(src, dst).wait_send()


def gather_kernel(
    outer, inner,
    x, cot, pos, vec, pq, pi, wo, wd,
    X, C, POS, VEC, WQ, WI, WO, WD, WDZ,
    loc, tok_s, tok_r, swap_s, swap_r, col_s, col_r, wd_s, wd_r,
):
    g, r = enter(outer, inner)
    swaps = [
        PlaneSwap(inner, g, r, lambda p: pq.at[p], lambda q: WQ.at[g, q], swap_s.at[0], swap_r.at[0]),
        PlaneSwap(inner, g, r, lambda p: vec, lambda q: VEC.at[g, q], swap_s.at[1], swap_r.at[1]),
        PlaneSwap(inner, g, r, lambda p: pi.at[p], lambda q: WI.at[g, q], swap_s.at[2], swap_r.at[2]),
        PlaneSwap(inner, g, r, lambda p: pos, lambda q: POS.at[q], swap_s.at[3], swap_r.at[3]),
    ]
    for swap in swaps[:3]:
        swap.start()
    own = [
        (pq.at[r], WQ.at[g, r]), (vec, VEC.at[g, r]), (pi.at[r], WI.at[g, r]),
        (pos, POS.at[r]), (x, X.at[r]), (cot, C.at[r]), (wo, WO.at[g]), (wd, WDZ.at[g]),
    ]
    own = [pltpu.make_async_copy(a, b, loc.at[i]) for i, (a, b) in enumerate(own)]
    for copy in own:
        copy.start()
    col_o = ColumnGather(outer, g, r, wo, WO, col_s.at[0], col_r.at[0])
    col_d = ColumnGather(outer, g, r, wd, WDZ, col_s.at[1], col_r.at[1])
    col_q = ColumnGather(outer, g, r, WQ.at[g], WQ, col_s.at[2], col_r.at[2])
    col_v = ColumnGather(outer, g, r, VEC.at[g], VEC, col_s.at[3], col_r.at[3])
    col_i = ColumnGather(outer, g, r, WI.at[g], WI, col_s.at[4], col_r.at[4])
    col_d.start()
    col_o.start()
    chips = inner // 2
    twin = r ^ 1
    by_a, by_b = r ^ 2, r ^ 4
    tok = lambda i, src, dst, to: remote(src, dst, tok_s.at[i], tok_r.at[i], g, to)
    first = [
        tok(0, x, X.at[r], by_a), tok(1, cot, C.at[r], by_b),
        tok(2, cot, C.at[r], by_a), tok(3, x, X.at[r], by_b),
    ]
    for copy in first:
        copy.start()
    swaps[3].start()
    pair = [tok(6, x, X.at[r], twin), tok(7, cot, C.at[r], twin)]
    for copy in pair:
        copy.start()
    for copy in own:
        copy.wait()
    for swap, col in zip(swaps[:3], (col_q, col_v, col_i)):
        swap.arrive()
        col.start()

    def pass_on(index, array, owner):
        copy = tok(index, array.at[owner], array.at[owner], twin)
        copy.start()
        pair.append(copy)

    tok(0, x, X.at[by_a], by_a).wait_recv()
    onward_a = tok(4, X.at[by_a], X.at[by_a], by_b)
    onward_a.start()
    pass_on(8, X, by_a)
    tok(1, cot, C.at[by_b], by_b).wait_recv()
    onward_b = tok(5, C.at[by_b], C.at[by_b], by_a)
    onward_b.start()
    pass_on(9, C, by_b)
    for col in (col_d, col_o, col_q, col_v, col_i):
        col.forward()
    tok(2, cot, C.at[by_a], by_a).wait_recv()
    pass_on(10, C, by_a)
    tok(3, x, X.at[by_b], by_b).wait_recv()
    pass_on(11, X, by_b)
    col_d.arrive()
    for z in range(outer):
        block = z * inner + r
        to, at = block // outer, lax.rem(block, outer)

        @pl.when(to == r)
        def _():
            copy = pltpu.make_async_copy(WDZ.at[z], WD.at[at], loc.at[0])
            copy.start()
            copy.wait()

        @pl.when(to != r)
        def _():
            remote(WDZ.at[z], WD.at[at], wd_s.at[z], wd_r.at[at], g, to).start()

    diag = r ^ 6
    tok(4, X.at[diag], X.at[diag], by_b).wait_recv()
    pass_on(12, X, diag)
    tok(5, C.at[diag], C.at[diag], by_a).wait_recv()
    pass_on(13, C, diag)
    swaps[3].arrive()
    for col in (col_o, col_q, col_v, col_i):
        col.arrive()
    for z in range(outer):
        source = lax.rem(r * outer + z, inner)
        to = (z * inner + r) // outer

        @pl.when(source != r)
        def _():
            remote(WD.at[z], WD.at[z], wd_s.at[z], wd_r.at[z], g, source).wait_recv()

        @pl.when(to != r)
        def _():
            remote(WDZ.at[z], WD.at[z], wd_s.at[z], wd_r.at[z], g, to).wait_send()

    for i, owner, array in (
        (6, twin, X), (7, twin, C), (8, twin ^ 2, X), (9, twin ^ 4, C),
        (10, twin ^ 2, C), (11, twin ^ 4, X), (12, twin ^ 6, X), (13, twin ^ 6, C),
    ):
        tok(i, array.at[owner], array.at[owner], twin).wait_recv()
    for copy in first + pair + [onward_a, onward_b]:
        copy.wait_send()
    for swap in swaps:
        swap.sent()
    for col in (col_d, col_o, col_q, col_v, col_i):
        col.sent()


def gather_all(outer, inner, x, cot, pos, vec, pq, pi, wo, wd):
    shape = jax.ShapeDtypeStruct
    dma = pltpu.SemaphoreType.DMA
    lead = lambda a, *n: shape((*n, *a.shape), a.dtype)
    cut = lambda a: shape((outer, *a.shape), a.dtype)
    any_spec = pl.BlockSpec(memory_space=pl.ANY)
    outs = (
        lead(x, inner), lead(cot, inner), lead(pos, inner), lead(vec, outer, inner),
        cut(pq), cut(pi), cut(wo), cut(wd), cut(wd),
    )
    return pl.pallas_call(
        functools.partial(gather_kernel, outer, inner),
        out_shape=outs,
        in_specs=[any_spec] * 8,
        out_specs=[any_spec] * 9,
        scratch_shapes=[
            dma((8,)), dma((14,)), dma((14,)), dma((4, inner)), dma((4, inner)),
            dma((5, outer + 1)), dma((5, outer + 1)), dma((outer,)), dma((outer,)),
        ],
        compiler_params=pltpu.CompilerParams(collective_id=0, has_side_effects=True),
    )(x, cot, pos, vec, pq, pi, wo, wd)


class ColumnSum:
    def __init__(self, outer, g, r, part, landing, send, recv):
        self.outer, self.g, self.r = outer, g, r
        self.part, self.landing, self.send, self.recv = part, landing, send, recv

    def copy(self, dst):
        return remote(
            self.part.at[dst], self.landing.at[self.g], self.send.at[dst],
            self.recv.at[self.g], dst, self.r,
        )

    def detour(self, dst, via):
        return remote(
            self.part.at[dst], self.landing.at[self.outer], self.send.at[dst],
            self.recv.at[self.outer], via, self.r,
        )

    def landed(self, slot):
        at = self.landing.at[slot]
        return remote(at, at, self.send.at[0], self.recv.at[slot], self.g, self.r)

    HOPS = ((0, 1, 3), (3, 2, 0))

    def start(self):
        if self.outer == 4:
            for src, via, dst in self.HOPS:
                @pl.when(self.g == src)
                def _(via=via, dst=dst):
                    self.detour(dst, via).start()
        for dst in range(self.outer):
            now = near(self.outer, self.g, dst)
            if self.outer == 4 and dst in (0, 3):
                now = now & (self.g != (1 if dst == 3 else 2))
            @pl.when(now)
            def _(dst=dst):
                self.copy(dst).start()

    def middle(self):
        if self.outer != 4:
            return
        for src, via, dst in self.HOPS:
            @pl.when(self.g == via)
            def _(dst=dst):
                self.landed(self.outer).wait_recv()
                mine = self.part[dst].astype(F32) + self.landing[self.outer].astype(F32)
                self.part[dst] = mine.astype(self.part.dtype)
                self.copy(dst).start()

    def total(self, out):
        out[...] = self.part[self.g].astype(F32)
        for src in range(self.outer):
            @pl.when(near(self.outer, self.g, src))
            def _(src=src):
                self.landed(src).wait_recv()
                out[...] += self.landing[src].astype(F32)

    def sent(self):
        for dst in range(self.outer):
            @pl.when(self.g != dst)
            def _(dst=dst):
                self.copy(dst).wait_send()


class PlaneSum:
    def __init__(self, inner, g, r, part, beside, mixed, landing, send, recv):
        self.chips, self.g, self.r = inner // 2, g, r
        self.part, self.beside, self.mixed, self.landing = part, beside, mixed, landing
        self.send, self.recv = send, recv

    def across(self, j):
        twin = self.r ^ 1
        return remote(
            self.part.at[twin ^ (2 * j)], self.beside.at[j], self.send.at[j],
            self.recv.at[j], self.g, twin,
        )

    def out(self, j):
        n = self.chips
        return remote(
            self.mixed.at[j], self.landing.at[j], self.send.at[n + j], self.recv.at[n + j],
            self.g, self.r ^ (2 * j),
        )

    def start(self):
        for j in range(self.chips - 1, -1, -1):
            self.across(j).start()

    def middle(self):
        for j in range(self.chips - 1, 0, -1):
            self.across(j).wait_recv()
            both = self.part[self.r ^ (2 * j)].astype(F32) + self.beside[j].astype(F32)
            self.mixed[j] = both.astype(BF)
            self.out(j).start()
        self.across(0).wait_recv()

    def total(self, out):
        out[...] = self.part[self.r].astype(F32) + self.beside[0].astype(F32)
        for j in range(1, self.chips):
            self.out(j).wait_recv()
            out[...] += self.landing[j].astype(F32)

    def sent(self):
        for j in range(self.chips):
            self.across(j).wait_send()
        for j in range(1, self.chips):
            self.out(j).wait_send()


def reduce_kernel(
    outer, inner,
    out_in, gn_in, gq_in, gi_in, go_in, gd_in, tab_in,
    out_f, gn_f, GQ, GI, go_f, gd_f, tab_f,
    out_p, gn_p, gq_p, gi_p, go_p, gd_p, tab_p,
    out_b, out_m, out_l, gn_b, gn_m, gn_l,
    gq_l, gi_l, go_l, gd_l, gd_z, gq_t, gi_t, gq_s, gi_s, tab_l, tab_z, tab_y,
    loc, pl_s, pl_r, col_s, col_r, swap_s, swap_r, gd_ss, gd_rs,
):
    g, r = enter(outer, inner)
    ins = (
        (gq_in, gq_p), (gi_in, gi_p), (go_in, go_p), (out_in, out_p), (gn_in, gn_p),
        (gd_in, gd_p), (tab_in, tab_p),
    )
    ins = [pltpu.make_async_copy(a, b, loc.at[i]) for i, (a, b) in enumerate(ins)]
    for copy in ins:
        copy.start()
    sum_q = ColumnSum(outer, g, r, gq_p, gq_l, col_s.at[0], col_r.at[0])
    sum_i = ColumnSum(outer, g, r, gi_p, gi_l, col_s.at[1], col_r.at[1])
    sum_o = ColumnSum(outer, g, r, go_p, go_l, col_s.at[2], col_r.at[2])
    sum_d = ColumnSum(outer, g, r, gd_z, gd_l, col_s.at[3], col_r.at[3])
    for copy, col in zip(ins[:3], (sum_q, sum_i, sum_o)):
        copy.wait()
        col.start()
    for copy in ins[3:]:
        copy.wait()
    plane_o = PlaneSum(inner, g, r, out_p, out_b, out_m, out_l, pl_s.at[0], pl_r.at[0])
    plane_n = PlaneSum(inner, g, r, gn_p, gn_b, gn_m, gn_l, pl_s.at[1], pl_r.at[1])
    for i in range(outer):
        block = r * outer + i
        z, to = block // inner, lax.rem(block, inner)

        @pl.when(to == r)
        def _():
            gd_z[z] = gd_p[i]

        @pl.when(to != r)
        def _():
            remote(gd_p.at[i], gd_z.at[z], gd_ss.at[i], gd_rs.at[z], g, to).start()

    tab_swap = PlaneSwap(
        inner, g, r, lambda p: tab_p.at[p], lambda q: tab_l.at[q], swap_s.at[0], swap_r.at[0]
    )
    tab_swap.start()
    plane_o.start()
    plane_n.start()
    for z in range(outer):
        source = (z * inner + r) // outer

        @pl.when(source != r)
        def _():
            remote(gd_z.at[z], gd_z.at[z], gd_ss.at[z], gd_rs.at[z], g, source).wait_recv()

    sum_d.start()
    tab_l[r] = tab_p[r]
    tab_swap.arrive()
    tab_z[...] = jnp.sum(tab_l[...], axis=0)
    tab_sum = ColumnSum(outer, g, r, tab_z, tab_y, col_s.at[4], col_r.at[4])
    tab_sum.start()
    plane_o.middle()
    plane_n.middle()
    for col in (sum_q, sum_i, sum_o, sum_d, tab_sum):
        col.middle()
    plane_o.total(out_f)
    plane_n.total(gn_f)
    sum_q.total(gq_t)
    gq_s[...] = gq_t[...].astype(BF)
    swap_q = PlaneSwap(
        inner, g, r, lambda p: gq_s.at[p], lambda q: GQ.at[q], swap_s.at[1], swap_r.at[1]
    )
    swap_q.start()
    GQ[r] = gq_s[r]
    sum_i.total(gi_t)
    gi_s[...] = gi_t[...].astype(BF)
    swap_i = PlaneSwap(
        inner, g, r, lambda p: gi_s.at[p], lambda q: GI.at[q], swap_s.at[2], swap_r.at[2]
    )
    swap_i.start()
    GI[r] = gi_s[r]
    sum_o.total(go_f)
    sum_d.total(gd_f)
    tab_sum.total(tab_f)
    swap_q.arrive()
    swap_i.arrive()
    for i in range(outer):
        to = lax.rem(r * outer + i, inner)

        @pl.when(to != r)
        def _():
            remote(gd_p.at[i], gd_z.at[i], gd_ss.at[i], gd_rs.at[i], g, to).wait_send()

    for item in (plane_o, plane_n, sum_q, sum_i, sum_o, sum_d, tab_sum, tab_swap, swap_q, swap_i):
        item.sent()


def reduce_all(outer, inner, out, gn, gq, gi, go, gd, tab):
    shape = jax.ShapeDtypeStruct
    dma = pltpu.SemaphoreType.DMA
    any_spec = pl.BlockSpec(memory_space=pl.ANY)
    vmem = pl.BlockSpec(memory_space=pltpu.VMEM)
    rows = out.shape[1:]
    outs = (
        shape(rows, F32), shape(rows, F32), shape(gq.shape[1:], BF), shape(gi.shape[1:], BF),
        shape(go.shape[1:], F32), shape(gd.shape[1:], F32), shape(tab.shape[2:], F32),
    )
    ins = (out, gn, gq, gi, go, gd, tab)
    like = lambda a: pltpu.VMEM(a.shape, a.dtype)
    more = lambda a: pltpu.VMEM((outer + 1, *a.shape[1:]), a.dtype)
    chips = inner // 2
    quad = pltpu.VMEM((chips, *rows), BF)
    scratch = [like(a) for a in ins] + [quad] * 6 + [
        more(gq), more(gi), more(go), more(gd), like(gd),
        pltpu.VMEM(gq.shape[1:], F32), pltpu.VMEM(gi.shape[1:], F32),
        pltpu.VMEM(gq.shape[1:], BF), pltpu.VMEM(gi.shape[1:], BF),
        like(tab), pltpu.VMEM(tab.shape[1:], F32), pltpu.VMEM((outer + 1, *tab.shape[2:]), F32),
        dma((7,)), dma((2, 2 * chips)), dma((2, 2 * chips)), dma((5, outer + 1)),
        dma((5, outer + 1)), dma((3, inner)), dma((3, inner)), dma((outer,)), dma((outer,)),
    ]
    return pl.pallas_call(
        functools.partial(reduce_kernel, outer, inner),
        out_shape=outs,
        in_specs=[any_spec] * 7,
        out_specs=[vmem] * 7,
        scratch_shapes=scratch,
        compiler_params=pltpu.CompilerParams(
            collective_id=1, has_side_effects=True, vmem_limit_bytes=VMEM_LIMIT
        ),
    )(*ins)


def attention_kernel(pos, q, k, v, gc, ctx, gq, gk, gv):
    block = BLOCK
    span = block + REACH
    gk[...] = jnp.zeros_like(gk)
    gv[...] = jnp.zeros_like(gv)
    nt = (((1,), (1,)), ((), ()))
    nn = (((1,), (0,)), ((), ()))
    tn = (((0,), (0,)), ((), ()))
    dot = functools.partial(lax.dot_general, preferred_element_type=F32)

    def step(i, carry):
        base = pl.multiple_of(i * block, block)
        reach = pos[i]
        spread = (
            lax.broadcasted_iota(jnp.int32, (span, block), 1) + REACH
            - lax.broadcasted_iota(jnp.int32, (span, block), 0)
        )
        allowed = (spread >= 0) & (spread <= reach)
        rows = pl.ds(base, block)
        keys = pl.ds(base, span)
        ctx_h, gq_h, gk_h, gv_h = [], [], [], []
        for h in range(q.shape[1] // HD):
            lanes = slice(h * HD, (h + 1) * HD)
            q_h, gc_h = q[rows, lanes], gc[rows, lanes]
            k_h, v_h = k[keys, lanes], v[keys, lanes]
            scores = jnp.where(allowed, dot(k_h, q_h, nt) * HD ** (-0.5), -1e30)
            top = jnp.max(scores, axis=0, keepdims=True)
            weight = jnp.exp(scores - top)
            probs = weight * (1.0 / jnp.sum(weight, axis=0, keepdims=True))
            probs_b = probs.astype(BF)
            ctx_h.append(dot(probs_b, v_h, tn))
            grad_probs = dot(v_h, gc_h, nt)
            row_dot = jnp.sum(probs * grad_probs, axis=0, keepdims=True)
            grad_s = (probs * (grad_probs - row_dot) * HD ** (-0.5)).astype(BF)
            gq_h.append(dot(grad_s, k_h, tn))
            gk_h.append(dot(grad_s, q_h, nn))
            gv_h.append(dot(probs_b, gc_h, nn))
        ctx[rows, :] = jnp.concatenate(ctx_h, axis=1).astype(BF)
        gq[rows, :] = jnp.concatenate(gq_h, axis=1)
        gk[keys, :] += jnp.concatenate(gk_h, axis=1)
        gv[keys, :] += jnp.concatenate(gv_h, axis=1)
        return carry

    lax.fori_loop(0, q.shape[0] // block, step, 0)


def attention(pos, q, k, v, gc):
    shape = jax.ShapeDtypeStruct
    rows, share = q.shape
    vmem = pl.BlockSpec(memory_space=pltpu.VMEM)
    flops = 7 * 2 * rows * (BLOCK + REACH) * share
    return pl.pallas_call(
        attention_kernel,
        out_shape=(
            shape(q.shape, BF), shape(q.shape, F32), shape(k.shape, F32), shape(k.shape, F32),
        ),
        in_specs=[vmem] * 5,
        out_specs=[vmem] * 4,
        compiler_params=pltpu.CompilerParams(vmem_limit_bytes=VMEM_LIMIT),
        cost_estimate=pl.CostEstimate(
            flops=flops, bytes_accessed=20 * rows * share, transcendentals=flops // (14 * HD)
        ),
    )(pos.reshape(rows // BLOCK, 1, BLOCK), q, k, v, gc)


def body(
    layer_input,
    ln1_gain,
    ln1_bias,
    qkv_weight,
    qkv_bias,
    dense_weight,
    dense_bias,
    ln2_gain,
    ln2_bias,
    fc_in_weight,
    fc_in_bias,
    fc_out_weight,
    fc_out_bias,
    positions,
    cotangent,
):
    bf = jnp.bfloat16
    f32 = jnp.float32
    outer = lax.axis_size("g")
    inner = lax.axis_size("r")
    count = outer * inner
    rank = lax.axis_index("r")
    tok_rows, width = layer_input.shape
    part_rows = qkv_weight.shape[0]
    share = width // inner
    unit = fc_out_weight.shape[0]
    hidden = outer * unit
    rows = inner * tok_rows

    vectors = [ln1_gain, ln1_bias, ln2_gain, ln2_bias, dense_bias, fc_out_bias, qkv_bias, fc_in_bias]
    sizes = [v.shape[0] for v in vectors]
    flat = jnp.concatenate(vectors)
    flat = jnp.pad(flat, (0, 2048 - flat.shape[0])).reshape(16, 128)
    pos = jnp.pad(positions, (0, 1024 - tok_rows)).reshape(8, 128)
    pq = (
        qkv_weight.reshape(part_rows, 3, inner, share)
        .transpose(2, 0, 1, 3)
        .reshape(inner, part_rows, 3 * share)
    )
    pi = (
        fc_in_weight.reshape(part_rows, outer, inner, unit)
        .transpose(2, 0, 1, 3)
        .reshape(inner, part_rows, hidden)
    )
    X, C, POS, VEC, WQ, WI, WO, WD, _ = gather_all(
        outer, inner, layer_input, cotangent, pos, flat, pq, pi, fc_out_weight, dense_weight
    )
    group_in = X.reshape(rows, width)
    group_top = C.reshape(rows, width)
    group_pos = POS.reshape(inner, 1024)[:, :tok_rows].reshape(rows)
    w_qkv = WQ.reshape(width, 3 * share)
    w_in = WI.reshape(width, hidden)
    w_out = WO.reshape(hidden, width)
    w_dense = WD.reshape(share, width)
    flat = VEC.reshape(count, 2048)
    full = []
    start = 0
    for size in sizes:
        full.append(flat[:, start : start + size].reshape(count * size).astype(f32))
        start += size
    gain_one, shift_one, gain_two, shift_two, bias_dense, bias_out, bias_qkv, bias_in = full
    bias_qkv = lax.dynamic_index_in_dim(bias_qkv.reshape(3, inner, share), rank, 1, False).reshape(-1)
    bias_in = lax.dynamic_index_in_dim(bias_in.reshape(outer, inner, unit), rank, 1, False).reshape(-1)

    normed, _ = norm_stats(group_in)
    left_attn = (normed * gain_one + shift_one).astype(bf)
    left_mlp = (normed * gain_two + shift_two).astype(bf)

    mixed_qkv = jnp.dot(left_attn, w_qkv, preferred_element_type=f32) + bias_qkv
    tables = rotary_tables(group_pos, 2 * share)
    rotated = rotate(mixed_qkv[:, : 2 * share], tables, 1.0).astype(bf)
    queries = rotated[:, :share]
    kv_own = jnp.concatenate([rotated[:, share:], mixed_qkv[:, 2 * share :].astype(bf)], axis=1)
    onward = [(i, i + 1) for i in range(outer - 1)]
    halo = lax.ppermute(kv_own[rows - REACH :], "g", onward)

    pre_act = jnp.dot(left_mlp, w_in, preferred_element_type=f32) + bias_in
    activated, gelu_slope = gelu_pair(pre_act)
    activated_b = activated.astype(bf)
    mlp_out = jnp.dot(activated_b, w_out, preferred_element_type=f32)
    grad_pre = times_transpose(group_top, w_out) * gelu_slope
    grad_pre_b = grad_pre.astype(bf)
    g_out_w = row_sum_product(activated_b, group_top).astype(bf)
    g_in_w = row_sum_product(left_mlp, grad_pre_b).astype(bf)
    g_in_b = jnp.sum(grad_pre, axis=0)
    grad_left_mlp = times_transpose(grad_pre_b, w_in)

    grad_context = times_transpose(group_top, w_dense).astype(bf)
    reach = jnp.concatenate([halo, kv_own], axis=0)
    context_b, g_q, g_k, g_v = attention(
        group_pos, queries, reach[:, :share], reach[:, share:], grad_context
    )
    attn_out = jnp.dot(context_b, w_dense, preferred_element_type=f32)
    out_part = (attn_out + mlp_out).astype(bf)
    g_dense_w = row_sum_product(context_b, group_top).astype(bf)
    g_kv = jnp.concatenate([g_k, g_v], axis=1)
    back = [(i + 1, i) for i in range(outer - 1)]
    returned = lax.ppermute(g_kv[:REACH].astype(bf), "g", back).astype(f32)
    g_kv = g_kv[REACH:] + jnp.pad(returned, ((rows - REACH, 0), (0, 0)))
    g_qk = rotate(jnp.concatenate([g_q, g_kv[:, :share]], axis=1), tables, -1.0)
    grad_qkv = jnp.concatenate([g_qk, g_kv[:, share:]], axis=1)
    grad_qkv_b = grad_qkv.astype(bf)
    g_qkv_w = row_sum_product(left_attn, grad_qkv_b).astype(bf)
    g_qkv_b = jnp.sum(grad_qkv, axis=0)
    grad_left_attn = times_transpose(grad_qkv_b, w_qkv)
    grad_normed = (grad_left_attn * gain_one + grad_left_mlp * gain_two).astype(bf)

    mine = (jnp.arange(inner) == rank).astype(f32)
    top_f = cotangent.astype(f32)
    sums = [
        jnp.sum(grad_left_attn * normed, axis=0),
        jnp.sum(grad_left_attn, axis=0),
        jnp.sum(grad_left_mlp * normed, axis=0),
        jnp.sum(grad_left_mlp, axis=0),
        jnp.sum(top_f, axis=0),
        (g_qkv_b.reshape(3, 1, share) * mine[None, :, None]).reshape(-1),
        (g_in_b.reshape(outer, 1, unit) * mine[None, :, None]).reshape(-1),
    ]
    lengths = [s.shape[0] // count for s in sums]
    table = jnp.concatenate([s.reshape(count, -1) for s in sums], axis=1)
    table = jnp.pad(table, ((0, 0), (0, 1024 - table.shape[1])))
    table = table.reshape(outer, inner, 8, 128).transpose(1, 0, 2, 3)

    out_sum, grad_normed, GQ, GI, g_out_w, g_dense_w, table = reduce_all(
        outer, inner,
        out_part.reshape(inner, tok_rows, width),
        grad_normed.reshape(inner, tok_rows, width),
        g_qkv_w.reshape(outer, inner, part_rows, 3 * share),
        g_in_w.reshape(outer, inner, part_rows, hidden),
        g_out_w.reshape(outer, unit, width),
        g_dense_w.reshape(outer, part_rows, width),
        table,
    )
    result = (layer_input.astype(f32) + out_sum + (bias_dense + bias_out)).astype(bf)
    g_qkv_w = (
        GQ.reshape(inner, part_rows, 3, share)
        .transpose(1, 2, 0, 3)
        .reshape(part_rows, 3 * width)
        .astype(f32)
    )
    g_in_w = (
        GI.reshape(inner, part_rows, outer, unit)
        .transpose(1, 2, 0, 3)
        .reshape(part_rows, count * unit)
        .astype(f32)
    )
    table = table.reshape(-1)
    out = []
    start = 0
    for length in lengths:
        out.append(table[start : start + length])
        start += length

    own_normed, inv_scale = norm_stats(layer_input)
    grad_in = top_f + inv_scale * (
        grad_normed
        - jnp.mean(grad_normed, axis=-1, keepdims=True)
        - own_normed * jnp.mean(grad_normed * own_normed, axis=-1, keepdims=True)
    )
    return (
        result,
        grad_in,
        out[0],
        out[1],
        g_qkv_w,
        out[5],
        g_dense_w,
        out[4],
        out[2],
        out[3],
        g_in_w,
        out[6],
        g_out_w,
        out[4],
    )


def solution(mesh):
    inner = GROUP
    split = Mesh(mesh.devices.reshape(-1, inner), ("g", "r"))
    flat = P(("g", "r"))
    tall = P(("g", "r"), None)
    in_specs = (
        tall, flat, flat, tall, flat, tall, flat, flat, flat, tall, flat, tall, flat, flat, tall,
    )
    out_specs = (
        tall, tall, flat, flat, tall, flat, tall, flat, flat, flat, tall, flat, tall, flat,
    )
    return jax.shard_map(body, mesh=split, in_specs=in_specs, out_specs=out_specs, check_vma=False)
```

```python
import functools

import jax
import jax.numpy as jnp
from jax import lax
from jax.experimental import pallas as pl
from jax.experimental.pallas import tpu as pltpu
from jax.sharding import Mesh
from jax.sharding import PartitionSpec as P

HEADS = 16
HD = 64
ROT = 16
REACH = 512
GROUP = 8
BLOCK = 256
EPSILON = 1e-05
ROPE_BASE = 10000.0
MESH = pl.DeviceIdType.MESH
BF = jnp.bfloat16
F32 = jnp.float32
VMEM_LIMIT = 58 * 2**20


def norm_stats(inputs):
    values_f = inputs.astype(jnp.float32)
    centre = jnp.mean(values_f, axis=-1, keepdims=True)
    shifted = values_f - centre
    variance = jnp.mean(shifted * shifted, axis=-1, keepdims=True)
    inv_scale = lax.rsqrt(variance + EPSILON)
    return (shifted * inv_scale, inv_scale)


def rotary_tables(positions, lanes):
    place = jnp.arange(lanes, dtype=jnp.int32) % HD
    counter = (place % (ROT // 2)).astype(jnp.float32)
    frequency = ROPE_BASE ** (-2.0 * counter / ROT)
    frequency = jnp.where(place < ROT, frequency, 0.0)
    angles = positions.astype(jnp.float32)[:, None] * frequency[None, :]
    sine = jnp.sin(angles)
    lower = jnp.where(place < ROT // 2, -sine, 0.0)
    upper = jnp.where(place >= ROT // 2, sine, 0.0)
    return (jnp.cos(angles), lower, upper)


def rotate(rows, tables, orient):
    cosine, lower, upper = tables
    ahead = jnp.roll(rows, -(ROT // 2), axis=1)
    behind = jnp.roll(rows, ROT // 2, axis=1)
    return rows * cosine + orient * (ahead * lower + behind * upper)


def gelu_pair(pre_act):
    cumulative = 0.5 * (1.0 + lax.erf(pre_act * 0.7071067811865476))
    density = jnp.exp(-0.5 * pre_act * pre_act) * 0.3989422804014327
    return (pre_act * cumulative, cumulative + pre_act * density)


def row_sum_product(left_side, right_side):
    return lax.dot_general(
        left_side, right_side, (((0,), (0,)), ((), ())), preferred_element_type=jnp.float32
    )


def times_transpose(left_side, right_side):
    return lax.dot_general(
        left_side, right_side, (((1,), (1,)), ((), ())), preferred_element_type=jnp.float32
    )


def remote(src, dst, send, recv, g, r):
    return pltpu.make_async_remote_copy(
        src_ref=src, dst_ref=dst, send_sem=send, recv_sem=recv,
        device_id=(g, r), device_id_type=MESH,
    )


def enter(outer, inner):
    g, r = lax.axis_index("g"), lax.axis_index("r")
    bar = pltpu.get_barrier_semaphore()
    for j in range(1, inner):
        pl.semaphore_signal(bar, inc=1, device_id=(g, r ^ j), device_id_type=MESH)
    for k in range(1, outer):
        pl.semaphore_signal(
            bar, inc=1, device_id=(lax.rem(g + k, outer), r), device_id_type=MESH
        )
    pl.semaphore_wait(bar, inner + outer - 2)
    return g, r


class PlaneSwap:
    def __init__(self, inner, g, r, src, dst, send, recv):
        self.copies = [
            remote(src(r ^ j), dst(r), send.at[j], recv.at[j], g, r ^ j) for j in range(1, inner)
        ]
        self.landed = [
            remote(dst(r ^ j), dst(r ^ j), send.at[j], recv.at[j], g, r ^ j)
            for j in range(1, inner)
        ]

    def start(self):
        for copy in self.copies:
            copy.start()

    def arrive(self):
        for copy in self.landed:
            copy.wait_recv()

    def sent(self):
        for copy in self.copies:
            copy.wait_send()


def near(outer, g, other):
    if outer != 4:
        return g != other
    return (g != other) & (jnp.abs(g - other) <= 2)


class ColumnGather:
    def __init__(self, outer, g, r, own, full, send, recv):
        self.outer, self.g, self.r = outer, g, r
        self.own, self.full, self.send, self.recv = own, full, send, recv

    def copy(self, dst):
        return remote(
            self.own, self.full.at[self.g], self.send.at[dst], self.recv.at[self.g], dst, self.r
        )

    def onward(self, src, dst):
        return remote(
            self.full.at[src], self.full.at[src], self.send.at[self.outer],
            self.recv.at[src], dst, self.r,
        )

    def start(self):
        order = range(self.outer)
        for dst in order:
            @pl.when(near(self.outer, self.g, dst))
            def _(dst=dst):
                self.copy(dst).start()

    def forward(self):
        if self.outer != 4:
            return
        for via, src, dst in ((2, 0, 3), (1, 3, 0)):
            @pl.when(self.g == via)
            def _(src=src, dst=dst):
                self.onward(src, dst).wait_recv()
                self.onward(src, dst).start()

    def arrive(self):
        for src in range(self.outer):
            waits = self.g != src
            if self.outer == 4 and src in (0, 3):
                waits = waits & (self.g != (2 if src == 0 else 1))
            @pl.when(waits)
            def _(src=src):
                self.onward(src, src).wait_recv()

    def sent(self):
        for dst in range(self.outer):
            @pl.when(near(self.outer, self.g, dst))
            def _(dst=dst):
                self.copy(dst).wait_send()
        if self.outer == 4:
            for via, src, dst in ((2, 0, 3), (1, 3, 0)):
                @pl.when(self.g == via)
                def _(src=src, dst=dst):
                    self.onward(src, dst).wait_send()


def gather_kernel(
    outer, inner,
    x, cot, pos, vec, pq, wd,
    X, C, POS, VEC, WQ, WD, WDZ,
    loc, tok_s, tok_r, swap_s, swap_r, col_s, col_r, wd_s, wd_r,
):
    g, r = enter(outer, inner)
    swaps = [
        PlaneSwap(inner, g, r, lambda p: pq.at[p], lambda q: WQ.at[g, q], swap_s.at[0], swap_r.at[0]),
        PlaneSwap(inner, g, r, lambda p: vec, lambda q: VEC.at[g, q], swap_s.at[1], swap_r.at[1]),
        PlaneSwap(inner, g, r, lambda p: pos, lambda q: POS.at[q], swap_s.at[2], swap_r.at[2]),
    ]
    for swap in swaps[:2]:
        swap.start()
    own = [
        (pq.at[r], WQ.at[g, r]), (vec, VEC.at[g, r]),
        (pos, POS.at[r]), (x, X.at[r]), (cot, C.at[r]), (wd, WDZ.at[g]),
    ]
    own = [pltpu.make_async_copy(a, b, loc.at[i]) for i, (a, b) in enumerate(own)]
    for copy in own:
        copy.start()
    col_d = ColumnGather(outer, g, r, wd, WDZ, col_s.at[0], col_r.at[0])
    col_q = ColumnGather(outer, g, r, WQ.at[g], WQ, col_s.at[1], col_r.at[1])
    col_v = ColumnGather(outer, g, r, VEC.at[g], VEC, col_s.at[2], col_r.at[2])
    col_d.start()
    chips = inner // 2
    twin = r ^ 1
    by_a, by_b = r ^ 2, r ^ 4
    tok = lambda i, src, dst, to: remote(src, dst, tok_s.at[i], tok_r.at[i], g, to)
    first = [
        tok(0, x, X.at[r], by_a), tok(1, cot, C.at[r], by_b),
        tok(2, cot, C.at[r], by_a), tok(3, x, X.at[r], by_b),
    ]
    for copy in first:
        copy.start()
    swaps[2].start()
    pair = [tok(6, x, X.at[r], twin), tok(7, cot, C.at[r], twin)]
    for copy in pair:
        copy.start()
    for copy in own:
        copy.wait()
    for swap, col in zip(swaps[:2], (col_q, col_v)):
        swap.arrive()
        col.start()

    def pass_on(index, array, owner):
        copy = tok(index, array.at[owner], array.at[owner], twin)
        copy.start()
        pair.append(copy)

    tok(0, x, X.at[by_a], by_a).wait_recv()
    onward_a = tok(4, X.at[by_a], X.at[by_a], by_b)
    onward_a.start()
    pass_on(8, X, by_a)
    tok(1, cot, C.at[by_b], by_b).wait_recv()
    onward_b = tok(5, C.at[by_b], C.at[by_b], by_a)
    onward_b.start()
    pass_on(9, C, by_b)
    for col in (col_d, col_q, col_v):
        col.forward()
    tok(2, cot, C.at[by_a], by_a).wait_recv()
    pass_on(10, C, by_a)
    tok(3, x, X.at[by_b], by_b).wait_recv()
    pass_on(11, X, by_b)
    col_d.arrive()
    for z in range(outer):
        block = z * inner + r
        to, at = block // outer, lax.rem(block, outer)

        @pl.when(to == r)
        def _():
            copy = pltpu.make_async_copy(WDZ.at[z], WD.at[at], loc.at[0])
            copy.start()
            copy.wait()

        @pl.when(to != r)
        def _():
            remote(WDZ.at[z], WD.at[at], wd_s.at[z], wd_r.at[at], g, to).start()

    diag = r ^ 6
    tok(4, X.at[diag], X.at[diag], by_b).wait_recv()
    pass_on(12, X, diag)
    tok(5, C.at[diag], C.at[diag], by_a).wait_recv()
    pass_on(13, C, diag)
    swaps[2].arrive()
    for col in (col_q, col_v):
        col.arrive()
    for z in range(outer):
        source = lax.rem(r * outer + z, inner)
        to = (z * inner + r) // outer

        @pl.when(source != r)
        def _():
            remote(WD.at[z], WD.at[z], wd_s.at[z], wd_r.at[z], g, source).wait_recv()

        @pl.when(to != r)
        def _():
            remote(WDZ.at[z], WD.at[z], wd_s.at[z], wd_r.at[z], g, to).wait_send()

    for i, owner, array in (
        (6, twin, X), (7, twin, C), (8, twin ^ 2, X), (9, twin ^ 4, C),
        (10, twin ^ 2, C), (11, twin ^ 4, X), (12, twin ^ 6, X), (13, twin ^ 6, C),
    ):
        tok(i, array.at[owner], array.at[owner], twin).wait_recv()
    for copy in first + pair + [onward_a, onward_b]:
        copy.wait_send()
    for swap in swaps:
        swap.sent()
    for col in (col_d, col_q, col_v):
        col.sent()


def gather_all(outer, inner, x, cot, pos, vec, pq, wd):
    shape = jax.ShapeDtypeStruct
    dma = pltpu.SemaphoreType.DMA
    lead = lambda a, *n: shape((*n, *a.shape), a.dtype)
    cut = lambda a: shape((outer, *a.shape), a.dtype)
    any_spec = pl.BlockSpec(memory_space=pl.ANY)
    outs = (
        lead(x, inner), lead(cot, inner), lead(pos, inner), lead(vec, outer, inner),
        cut(pq), cut(wd), cut(wd),
    )
    return pl.pallas_call(
        functools.partial(gather_kernel, outer, inner),
        out_shape=outs,
        in_specs=[any_spec] * 6,
        out_specs=[any_spec] * 7,
        scratch_shapes=[
            dma((6,)), dma((14,)), dma((14,)), dma((3, inner)), dma((3, inner)),
            dma((3, outer + 1)), dma((3, outer + 1)), dma((outer,)), dma((outer,)),
        ],
        compiler_params=pltpu.CompilerParams(collective_id=0, has_side_effects=True),
    )(x, cot, pos, vec, pq, wd)


class ColumnSum:
    def __init__(self, outer, g, r, part, landing, send, recv):
        self.outer, self.g, self.r = outer, g, r
        self.part, self.landing, self.send, self.recv = part, landing, send, recv

    def copy(self, dst):
        return remote(
            self.part.at[dst], self.landing.at[self.g], self.send.at[dst],
            self.recv.at[self.g], dst, self.r,
        )

    def detour(self, dst, via):
        return remote(
            self.part.at[dst], self.landing.at[self.outer], self.send.at[dst],
            self.recv.at[self.outer], via, self.r,
        )

    def landed(self, slot):
        at = self.landing.at[slot]
        return remote(at, at, self.send.at[0], self.recv.at[slot], self.g, self.r)

    HOPS = ((0, 1, 3), (3, 2, 0))

    def start(self):
        if self.outer == 4:
            for src, via, dst in self.HOPS:
                @pl.when(self.g == src)
                def _(via=via, dst=dst):
                    self.detour(dst, via).start()
        for dst in range(self.outer):
            now = near(self.outer, self.g, dst)
            if self.outer == 4 and dst in (0, 3):
                now = now & (self.g != (1 if dst == 3 else 2))
            @pl.when(now)
            def _(dst=dst):
                self.copy(dst).start()

    def middle(self):
        if self.outer != 4:
            return
        for src, via, dst in self.HOPS:
            @pl.when(self.g == via)
            def _(dst=dst):
                self.landed(self.outer).wait_recv()
                both = self.part[dst].astype(F32) + self.landing[self.outer].astype(F32)
                self.landing[self.outer] = both.astype(self.landing.dtype)
                at = self.landing.at
                remote(
                    at[self.outer], at[self.g], self.send.at[dst], self.recv.at[self.g],
                    dst, self.r,
                ).start()

    def total(self, out):
        out[...] = self.part[self.g].astype(F32)
        for src in range(self.outer):
            @pl.when(near(self.outer, self.g, src))
            def _(src=src):
                self.landed(src).wait_recv()
                out[...] += self.landing[src].astype(F32)

    def sent(self):
        for dst in range(self.outer):
            @pl.when(self.g != dst)
            def _(dst=dst):
                self.copy(dst).wait_send()


class PlaneSum:
    def __init__(self, inner, g, r, part, beside, mixed, landing, send, recv):
        self.chips, self.g, self.r = inner // 2, g, r
        self.part, self.beside, self.mixed, self.landing = part, beside, mixed, landing
        self.send, self.recv = send, recv

    def across(self, j):
        twin = self.r ^ 1
        return remote(
            self.part.at[twin ^ (2 * j)], self.beside.at[j], self.send.at[j],
            self.recv.at[j], self.g, twin,
        )

    def out(self, j):
        n = self.chips
        return remote(
            self.mixed.at[j], self.landing.at[j], self.send.at[n + j], self.recv.at[n + j],
            self.g, self.r ^ (2 * j),
        )

    def start(self):
        for j in range(self.chips - 1, -1, -1):
            self.across(j).start()

    def middle(self):
        for j in range(self.chips - 1, 0, -1):
            self.across(j).wait_recv()
            both = self.part[self.r ^ (2 * j)].astype(F32) + self.beside[j].astype(F32)
            self.mixed[j] = both.astype(BF)
            self.out(j).start()
        self.across(0).wait_recv()

    def total(self, out):
        out[...] = self.part[self.r].astype(F32) + self.beside[0].astype(F32)
        for j in range(1, self.chips):
            self.out(j).wait_recv()
            out[...] += self.landing[j].astype(F32)

    def sent(self):
        for j in range(self.chips):
            self.across(j).wait_send()
        for j in range(1, self.chips):
            self.out(j).wait_send()


NN = (((1,), (0,)), ((), ()))
NT = (((1,), (1,)), ((), ()))
TN = (((0,), (0,)), ((), ()))


def dot(left, right, dims):
    return lax.dot_general(left, right, dims, preferred_element_type=F32)


def column_sum(values):
    return jnp.sum(values, axis=0, keepdims=True)


def attention_kernel(
    outer, inner,
    X, C, WQ, WD, pos, vecs, bq, pi, wo,
    LM, AP, GN, GQW, GDW, SUMS, QB, WI, WO,
    la, q, gc, kk, vv, gq, gk, gv, ctx, gb, cosine, lower, upper, back, away,
    loc, swap_s, swap_r, col_s, col_r, halo_s, halo_r,
):
    g, r = enter(outer, inner)
    swap_i = PlaneSwap(
        inner, g, r, lambda p: pi.at[p], lambda o: WI.at[g, o], swap_s, swap_r
    )
    swap_i.start()
    own = [
        pltpu.make_async_copy(wo, WO.at[g], loc.at[0]),
        pltpu.make_async_copy(pi.at[r], WI.at[g, r], loc.at[1]),
    ]
    for copy in own:
        copy.start()
    col_o = ColumnGather(outer, g, r, wo, WO, col_s.at[0], col_r.at[0])
    col_i = ColumnGather(outer, g, r, WI.at[g], WI, col_s.at[1], col_r.at[1])
    col_o.start()

    rows, share = q.shape
    block = BLOCK
    span = block + REACH
    count = rows // block
    tail = REACH // block
    half = ROT // 2
    step_of = lax.broadcasted_iota(jnp.int32, (half, rows), 0).astype(F32)
    angles = pos[...] * jnp.exp(step_of * (-2.0 / ROT * jnp.log(ROPE_BASE)))
    cos_t, sin_t = jnp.cos(angles), jnp.sin(angles)
    heads = share // HD
    rest = HD - ROT
    blank = jnp.zeros((half, rows), F32)
    quiet = jnp.zeros((rest, rows), F32)
    tall = lambda parts: jnp.transpose(jnp.concatenate(parts * heads, axis=0))
    cosine[...] = tall([cos_t, cos_t, quiet + 1.0])
    lower[...] = tall([-sin_t, blank, quiet])
    upper[...] = tall([blank, sin_t, quiet])

    def turn(values, at, orient):
        ahead = pltpu.roll(values, share - half, 1)
        behind = pltpu.roll(values, half, 1)
        return values * cosine[at, :] + orient * (ahead * lower[at, :] + behind * upper[at, :])

    def chunk(i):
        return pl.ds(pl.multiple_of(i * block, block), block)

    def ahead(i):
        return pl.ds(pl.multiple_of(i * block + REACH, block), block)

    def project(j, carry):
        i = count - 1 - j
        at = chunk(i)
        normed, _ = norm_stats(X[at, :])
        left = (normed * vecs[0:1, :] + vecs[1:2, :]).astype(BF)
        la[at, :] = left
        LM[at, :] = (normed * vecs[2:3, :] + vecs[3:4, :]).astype(BF)
        mixed = dot(left, WQ[...], NN) + bq[...]
        q[at, :] = turn(mixed[:, :share], at, 1.0).astype(BF)
        kk[ahead(i), :] = turn(mixed[:, share : 2 * share], at, 1.0).astype(BF)
        vv[ahead(i), :] = mixed[:, 2 * share :].astype(BF)
        gc[at, :] = dot(C[at, :], WD[...], NT).astype(BF)
        return carry

    first, last = pl.ds(0, REACH), pl.ds(rows, REACH)

    def halo(n, src, dst, to):
        return remote(src, dst, halo_s.at[n], halo_r.at[n], to, r)

    lax.fori_loop(0, tail, project, 0)

    @pl.when(g < outer - 1)
    def _():
        halo(0, kk.at[last], kk.at[first], g + 1).start()
        halo(1, vv.at[last], vv.at[first], g + 1).start()

    @pl.when(g == 0)
    def _():
        kk[first, :] = jnp.zeros((REACH, share), BF)
        vv[first, :] = jnp.zeros((REACH, share), BF)

    lax.fori_loop(tail, count, project, 0)
    for copy in own:
        copy.wait()
    swap_i.arrive()
    col_i.start()
    gk[...] = jnp.zeros_like(gk)
    gv[...] = jnp.zeros_like(gv)

    def attend(i, carry):
        at = chunk(i)
        keys = pl.ds(pl.multiple_of(i * block, block), span)
        reach = pos[:, at].astype(jnp.int32)
        spread = (
            lax.broadcasted_iota(jnp.int32, (span, block), 1) + REACH
            - lax.broadcasted_iota(jnp.int32, (span, block), 0)
        )
        allowed = (spread >= 0) & (spread <= reach)
        ctx_h, gq_h, gk_h, gv_h = [], [], [], []
        for h in range(heads):
            lanes = slice(h * HD, (h + 1) * HD)
            q_h, gc_h = q[at, lanes], gc[at, lanes]
            k_h, v_h = kk[keys, lanes], vv[keys, lanes]
            scores = jnp.where(allowed, dot(k_h, q_h, NT) * HD ** (-0.5), -1e30)
            top = jnp.max(scores, axis=0, keepdims=True)
            weight = jnp.exp(scores - top)
            probs = weight * (1.0 / jnp.sum(weight, axis=0, keepdims=True))
            probs_b = probs.astype(BF)
            ctx_h.append(dot(probs_b, v_h, TN))
            grad_probs = dot(v_h, gc_h, NT)
            row_dot = jnp.sum(probs * grad_probs, axis=0, keepdims=True)
            grad_s = (probs * (grad_probs - row_dot) * HD ** (-0.5)).astype(BF)
            gq_h.append(dot(grad_s, k_h, TN))
            gk_h.append(dot(grad_s, q_h, NN))
            gv_h.append(dot(probs_b, gc_h, NN))
        ctx[at, :] = jnp.concatenate(ctx_h, axis=1).astype(BF)
        gq[at, :] = jnp.concatenate(gq_h, axis=1)
        gk[keys, :] += jnp.concatenate(gk_h, axis=1)
        gv[keys, :] += jnp.concatenate(gv_h, axis=1)
        return carry

    lax.fori_loop(tail, count, attend, 0)

    @pl.when(g > 0)
    def _():
        halo(0, kk.at[first], kk.at[first], g).wait_recv()
        halo(1, vv.at[first], vv.at[first], g).wait_recv()

    lax.fori_loop(0, tail, attend, 0)
    away[0] = gk[first, :].astype(BF)
    away[1] = gv[first, :].astype(BF)

    @pl.when(g > 0)
    def _():
        halo(2, away, back, g - 1).start()

    @pl.when(g == outer - 1)
    def _():
        back[...] = jnp.zeros_like(back)

    col_o.forward()
    SUMS[...] = jnp.zeros_like(SUMS)
    QB[...] = jnp.zeros_like(QB)

    def finish(i, carry):
        at = chunk(i)
        grads = jnp.concatenate(
            [
                turn(gq[at, :], at, -1.0), turn(gk[ahead(i), :], at, -1.0),
                gv[ahead(i), :],
            ],
            axis=1,
        )
        QB[0:1, :] += column_sum(grads)
        grads_b = grads.astype(BF)
        gb[at, :] = grads_b
        AP[at, :] = dot(ctx[at, :], WD[...], NN).astype(BF)
        grad_left = dot(grads_b, WQ[...], NT)
        normed, _ = norm_stats(X[at, :])
        SUMS[0:1, :] += column_sum(grad_left * normed)
        SUMS[1:2, :] += column_sum(grad_left)
        GN[at, :] = (grad_left * vecs[0:1, :]).astype(BF)
        return carry

    lax.fori_loop(0, count - tail, finish, 0)

    @pl.when(g < outer - 1)
    def _():
        halo(2, away, back, g).wait_recv()

    gk[last, :] += back[0].astype(F32)
    gv[last, :] += back[1].astype(F32)
    lax.fori_loop(count - tail, count, finish, 0)
    col_i.forward()

    def weights(n, carry):
        at = pl.ds(pl.multiple_of(n * 256, 256), 256)
        GQW[at, :] = dot(la[:, at], gb[...], TN).astype(BF)
        GDW[:, at] = dot(ctx[...], C[:, at], TN).astype(BF)
        return carry

    lax.fori_loop(0, la.shape[1] // 256, weights, 0)

    @pl.when(g < outer - 1)
    def _():
        halo(0, kk.at[last], kk.at[first], g).wait_send()
        halo(1, vv.at[last], vv.at[first], g).wait_send()

    @pl.when(g > 0)
    def _():
        halo(2, away, back, g).wait_send()

    for col in (col_o, col_i):
        col.arrive()
    for item in (swap_i, col_o, col_i):
        item.sent()


def attention(outer, inner, X, C, WQ, WD, pos, vecs, bq, pi, wo):
    shape = jax.ShapeDtypeStruct
    dma = pltpu.SemaphoreType.DMA
    vmem = pl.BlockSpec(memory_space=pltpu.VMEM)
    any_spec = pl.BlockSpec(memory_space=pl.ANY)
    rows, width = X.shape
    share = WD.shape[0]
    wide = shape((rows, width), BF)
    outs = (
        wide, wide, wide, shape(WQ.shape, BF), shape(WD.shape, BF), shape((8, width), F32),
        shape((8, 3 * share), F32), shape((outer, *pi.shape), BF), shape((outer, *wo.shape), BF),
    )
    own = (rows, share)
    more = (rows + REACH, share)
    v = pltpu.VMEM
    return pl.pallas_call(
        functools.partial(attention_kernel, outer, inner),
        out_shape=outs,
        in_specs=[vmem] * 7 + [any_spec] * 2,
        out_specs=[vmem] * 7 + [any_spec] * 2,
        scratch_shapes=[
            v((rows, width), BF), v(own, BF), v(own, BF), v(more, BF), v(more, BF),
            v(own, F32), v(more, F32), v(more, F32), v(own, BF), v((rows, 3 * share), BF),
            v(own, F32), v(own, F32), v(own, F32), v((2, REACH, share), BF),
            v((2, REACH, share), BF),
            dma((2,)), dma((inner,)), dma((inner,)), dma((2, outer + 1)), dma((2, outer + 1)),
            dma((3,)), dma((3,)),
        ],
        compiler_params=pltpu.CompilerParams(
            collective_id=1, has_side_effects=True, vmem_limit_bytes=VMEM_LIMIT
        ),
    )(X, C, WQ, WD, pos, vecs, bq, pi, wo)


def feed_kernel(
    outer, inner, neat,
    LM, C, X, AP, GN, WI, WO, vecs, bi, gq_p, gd_p, sums, top, qb,
    out_f, gn_f, GQ, GI, go_f, gd_f, TS,
    act, gp, out_p, gn_p, out_b, out_m, out_l, gn_b, gn_m, gn_l,
    gi_w, go_w, gi_l, go_l, gq_l, gd_l, gd_z, gq_t, gi_t, gq_s, gi_s, gq_e, gi_e,
    table, table_z,
    pl_s, pl_r, col_s, col_r, swap_s, swap_r, gd_ss, gd_rs,
):
    g, r = enter(outer, inner)
    sum_q = ColumnSum(outer, g, r, gq_p, gq_l, col_s.at[0], col_r.at[0])
    sum_i = ColumnSum(outer, g, r, gi_w, gi_l, col_s.at[1], col_r.at[1])
    sum_o = ColumnSum(outer, g, r, go_w, go_l, col_s.at[2], col_r.at[2])
    sum_d = ColumnSum(outer, g, r, gd_z, gd_l, col_s.at[3], col_r.at[3])
    sum_q.start()
    for i in range(outer):
        owner = r * outer + i
        z, to = owner // inner, lax.rem(owner, inner)

        @pl.when(to == r)
        def _():
            gd_z[z] = gd_p[i]

        @pl.when(to != r)
        def _():
            remote(gd_p.at[i], gd_z.at[z], gd_ss.at[i], gd_rs.at[z], g, to).start()

    rows, width = X.shape
    block = BLOCK
    hidden = bi.shape[1]
    count = rows // block
    table[...] = jnp.zeros_like(table)

    def chunk(i):
        return pl.ds(pl.multiple_of(i * block, block), block)

    def inside(i, carry):
        at = chunk(i)
        pre_act = dot(LM[at, :], WI[...], NN) + bi[...]
        activated, slope = gelu_pair(pre_act)
        act[at, :] = activated.astype(BF)
        grad_pre = dot(C[at, :], WO[...], NT) * slope
        gp[at, :] = grad_pre.astype(BF)
        table[6:7, :hidden] += column_sum(grad_pre)
        return carry

    lax.fori_loop(0, count, inside, 0)
    unit = go_w.shape[1]
    for t in range(outer):
        go_w[t] = dot(act[:, t * unit : (t + 1) * unit], C[...], TN).astype(BF)
    sum_o.start()
    part = gi_w.shape[1] * gi_w.shape[2]
    for t in range(outer):
        grad = dot(LM[:, t * part : (t + 1) * part], gp[...], TN).astype(BF)
        gi_w[t] = grad.reshape(gi_w.shape[1:])
    sum_i.start()
    for z in range(outer):
        source = (z * inner + r) // outer

        @pl.when(source != r)
        def _():
            remote(gd_z.at[z], gd_z.at[z], gd_ss.at[z], gd_rs.at[z], g, source).wait_recv()

    sum_d.start()

    tok_rows = out_p.shape[1]

    def outside(i, carry):
        at = pl.ds(pl.multiple_of(i * tok_rows, 16), tok_rows)
        mlp_out = dot(act[at, :], WO[...], NN)
        out_p[i] = (AP[at, :].astype(F32) + mlp_out).astype(BF)
        grad_left = dot(gp[at, :], WI[...], NT)
        normed, _ = norm_stats(X[at, :])
        table[2:3, :] += column_sum(grad_left * normed)
        table[3:4, :] += column_sum(grad_left)
        gn_p[i] = (GN[at, :].astype(F32) + grad_left * vecs[2:3, :]).astype(BF)
        return carry

    lax.fori_loop(0, inner, outside, 0)
    plane_o = PlaneSum(inner, g, r, out_p, out_b, out_m, out_l, pl_s.at[0], pl_r.at[0])
    plane_n = PlaneSum(inner, g, r, gn_p, gn_b, gn_m, gn_l, pl_s.at[1], pl_r.at[1])
    plane_n.start()
    plane_o.start()
    table[0:2, :] = sums[0:2, :]
    table[4:5, :] = column_sum(top[...].astype(F32))
    table[5:6, : qb.shape[1]] = qb[0:1, :]
    col_t = ColumnGather(outer, g, r, table, table_z, col_s.at[4], col_r.at[4])
    col_t.start()
    sum_q.middle()
    sum_o.middle()
    plane_n.middle()
    plane_o.middle()
    sum_i.middle()
    sum_d.middle()
    col_t.forward()
    sum_q.total(gq_t)
    gq_s[...] = gq_t[...].astype(BF)
    swap_q = PlaneSwap(
        inner, g, r, lambda p: gq_s.at[p], lambda o: gq_e.at[o], swap_s.at[0], swap_r.at[0]
    )
    swap_q.start()
    gq_e[r] = gq_s[r]
    col_t.arrive()
    table_z[g] = table[...]
    TS[r] = jnp.sum(table_z[: outer], axis=0)
    swap_t = PlaneSwap(
        inner, g, r, lambda p: TS.at[r], lambda o: TS.at[o], swap_s.at[1], swap_r.at[1]
    )
    swap_t.start()
    sum_o.total(go_f)
    sum_i.total(gi_t)
    gi_s[...] = gi_t[...].astype(BF)
    swap_i = PlaneSwap(
        inner, g, r, lambda p: gi_s.at[p], lambda o: gi_e.at[o], swap_s.at[2], swap_r.at[2]
    )
    swap_i.start()
    gi_e[r] = gi_s[r]
    sum_d.total(gd_f)
    plane_n.total(gn_f)
    plane_o.total(out_f)
    swap_q.arrive()
    swap_t.arrive()

    def settle(out, landed):
        if not neat:
            out[...] = landed[...]
            return
        parts = landed.shape[2] // 128
        for owner in range(inner):
            for n in range(parts):
                at = (n * inner + owner) * 128
                out[:, at : at + 128] = landed[owner][:, n * 128 : n * 128 + 128].astype(F32)

    settle(GQ, gq_e)
    swap_i.arrive()
    settle(GI, gi_e)
    for i in range(outer):
        to = lax.rem(r * outer + i, inner)

        @pl.when(to != r)
        def _():
            remote(gd_p.at[i], gd_z.at[i], gd_ss.at[i], gd_rs.at[i], g, to).wait_send()

    for item in (
        plane_o, plane_n, sum_q, sum_i, sum_o, sum_d, col_t, swap_q, swap_i, swap_t,
    ):
        item.sent()


def feed_forward(outer, inner, LM, C, X, AP, GN, WI, WO, vecs, bi, gq, gd, sums, top, qb):
    shape = jax.ShapeDtypeStruct
    dma = pltpu.SemaphoreType.DMA
    vmem = pl.BlockSpec(memory_space=pltpu.VMEM)
    rows, width = X.shape
    tok_rows = rows // inner
    hidden = bi.shape[1]
    part_rows = width // (outer * inner)
    unit = hidden // outer
    share = gq.shape[3] // 3
    neat = unit % 128 == 0 and share == 128 and part_rows % 16 == 0
    piece_q = (inner, part_rows, 3 * share)
    piece_i = (inner, part_rows, hidden)
    piece_o = (unit, width)
    piece_d = (part_rows, width)
    outs = (
        shape((tok_rows, width), F32), shape((tok_rows, width), F32),
        shape((part_rows, 3 * width), F32) if neat else shape(piece_q, BF),
        shape((part_rows, hidden * inner), F32) if neat else shape(piece_i, BF),
        shape(piece_o, F32), shape(piece_d, F32), shape((inner, 8, width), F32),
    )
    chips = inner // 2
    v = pltpu.VMEM
    quad = v((chips, tok_rows, width), BF)
    group = v((inner, tok_rows, width), BF)
    scratch = [
        v((rows, hidden), BF), v((rows, hidden), BF), group, group, *([quad] * 6),
        v((outer, *piece_i), BF), v((outer, *piece_o), BF),
        v((outer + 1, *piece_i), BF), v((outer + 1, *piece_o), BF),
        v((outer + 1, *piece_q), BF), v((outer + 1, *piece_d), BF), v((outer, *piece_d), BF),
        v(piece_q, F32), v(piece_i, F32), v(piece_q, BF), v(piece_i, BF),
        v(piece_q, BF), v(piece_i, BF), v((8, width), F32), v((outer, 8, width), F32),
        dma((2, 2 * chips)), dma((2, 2 * chips)), dma((5, outer + 1)), dma((5, outer + 1)),
        dma((3, inner)), dma((3, inner)), dma((outer,)), dma((outer,)),
    ]
    out = pl.pallas_call(
        functools.partial(feed_kernel, outer, inner, neat),
        out_shape=outs,
        in_specs=[vmem] * 14,
        out_specs=[vmem] * 7,
        scratch_shapes=scratch,
        compiler_params=pltpu.CompilerParams(
            collective_id=2, has_side_effects=True, vmem_limit_bytes=VMEM_LIMIT
        ),
    )(LM, C, X, AP, GN, WI, WO, vecs, bi, gq, gd, sums, top, qb)
    out = list(out)
    if not neat:
        for n, parts in ((2, 3), (3, outer)):
            out[n] = (
                out[n].reshape(inner, part_rows, parts, -1)
                .transpose(1, 2, 0, 3)
                .reshape(part_rows, -1)
                .astype(F32)
            )
    return out


def body(
    layer_input,
    ln1_gain,
    ln1_bias,
    qkv_weight,
    qkv_bias,
    dense_weight,
    dense_bias,
    ln2_gain,
    ln2_bias,
    fc_in_weight,
    fc_in_bias,
    fc_out_weight,
    fc_out_bias,
    positions,
    cotangent,
):
    bf = jnp.bfloat16
    f32 = jnp.float32
    outer = lax.axis_size("g")
    inner = lax.axis_size("r")
    count = outer * inner
    rank = lax.axis_index("r")
    tok_rows, width = layer_input.shape
    part_rows = qkv_weight.shape[0]
    share = width // inner
    unit = fc_out_weight.shape[0]
    hidden = outer * unit
    rows = inner * tok_rows

    vectors = [ln1_gain, ln1_bias, ln2_gain, ln2_bias, dense_bias, fc_out_bias, qkv_bias, fc_in_bias]
    sizes = [v.shape[0] for v in vectors]
    flat = jnp.concatenate(
        [jnp.pad(v.astype(f32)[None], ((0, 0), (0, 128 - v.shape[0]))) for v in vectors], axis=0
    )
    pos = jnp.pad(positions, (0, 1024 - tok_rows)).reshape(8, 128)
    pq = (
        qkv_weight.reshape(part_rows, 3, inner, share)
        .transpose(2, 0, 1, 3)
        .reshape(inner, part_rows, 3 * share)
    )
    pi = (
        fc_in_weight.reshape(part_rows, outer, inner, unit)
        .transpose(2, 0, 1, 3)
        .reshape(inner, part_rows, hidden)
    )
    X, C, POS, VEC, WQ, WD, _ = gather_all(
        outer, inner, layer_input, cotangent, pos, flat, pq, dense_weight
    )
    group_in = X.reshape(rows, width)
    group_top = C.reshape(rows, width)
    group_pos = POS.reshape(inner, 1024)[:, :tok_rows].reshape(1, rows).astype(f32)
    full = [
        VEC[:, :, n, :size].reshape(count * size) for n, size in enumerate(sizes)
    ]
    gain_one, shift_one, gain_two, shift_two, bias_dense, bias_out, bias_qkv, bias_in = full
    bias_qkv = lax.dynamic_index_in_dim(bias_qkv.reshape(3, inner, share), rank, 1, False)
    bias_in = lax.dynamic_index_in_dim(bias_in.reshape(outer, inner, unit), rank, 1, False)
    vecs = jnp.stack([gain_one, shift_one, gain_two, shift_two] * 2)
    LM, AP, GN, GQW, GDW, SUMS, QB, WI, WO = attention(
        outer, inner, group_in, group_top, WQ.reshape(width, 3 * share),
        WD.reshape(share, width), group_pos, vecs, bias_qkv.reshape(1, -1), pi, fc_out_weight,
    )
    out_sum, grad_normed, g_qkv_w, g_in_w, g_out_w, g_dense_w, table = feed_forward(
        outer, inner, LM, group_top, group_in, AP, GN, WI.reshape(width, hidden),
        WO.reshape(hidden, width), vecs, bias_in.reshape(1, -1),
        GQW.reshape(outer, inner, part_rows, 3 * share),
        GDW.reshape(outer, part_rows, width), SUMS, cotangent, QB,
    )
    result = (layer_input.astype(f32) + out_sum + (bias_dense + bias_out)).astype(bf)
    device = lax.axis_index("g") * inner + rank
    own = lax.dynamic_slice_in_dim(
        jnp.sum(table[:, :5], axis=0), device * part_rows, part_rows, axis=1
    )
    out = [own[n] for n in range(5)]
    for n, lanes, parts in ((5, 3 * share, 3), (6, hidden, outer)):
        vector = table[:, n, :lanes].reshape(inner, parts, -1).transpose(1, 0, 2).reshape(-1)
        size = vector.shape[0] // count
        out.append(lax.dynamic_slice_in_dim(vector, device * size, size))
    top_f = cotangent.astype(f32)

    own_normed, inv_scale = norm_stats(layer_input)
    grad_in = top_f + inv_scale * (
        grad_normed
        - jnp.mean(grad_normed, axis=-1, keepdims=True)
        - own_normed * jnp.mean(grad_normed * own_normed, axis=-1, keepdims=True)
    )
    return (
        result,
        grad_in,
        out[0],
        out[1],
        g_qkv_w,
        out[5],
        g_dense_w,
        out[4],
        out[2],
        out[3],
        g_in_w,
        out[6],
        g_out_w,
        out[4],
    )


def solution(mesh):
    inner = GROUP
    split = Mesh(mesh.devices.reshape(-1, inner), ("g", "r"))
    flat = P(("g", "r"))
    tall = P(("g", "r"), None)
    in_specs = (
        tall, flat, flat, tall, flat, tall, flat, flat, flat, tall, flat, tall, flat, flat, tall,
    )
    out_specs = (
        tall, tall, flat, flat, tall, flat, tall, flat, flat, flat, tall, flat, tall, flat,
    )
    return jax.shard_map(body, mesh=split, in_specs=in_specs, out_specs=out_specs, check_vma=False)
```

```python
import functools

import jax
import jax.numpy as jnp
from jax import lax
from jax.experimental import pallas as pl
from jax.experimental.pallas import tpu as pltpu
from jax.sharding import Mesh
from jax.sharding import PartitionSpec as P

HEADS = 16
HD = 64
ROT = 16
REACH = 512
GROUP = 8
BLOCK = 256
EPSILON = 1e-05
ROPE_BASE = 10000.0
MESH = pl.DeviceIdType.MESH
BF = jnp.bfloat16
F32 = jnp.float32
VMEM_LIMIT = 60 * 2**20


def norm_stats(inputs):
    values_f = inputs.astype(jnp.float32)
    centre = jnp.mean(values_f, axis=-1, keepdims=True)
    shifted = values_f - centre
    variance = jnp.mean(shifted * shifted, axis=-1, keepdims=True)
    inv_scale = lax.rsqrt(variance + EPSILON)
    return (shifted * inv_scale, inv_scale)


def gelu_pair(pre_act):
    cumulative = 0.5 * (1.0 + lax.erf(pre_act * 0.7071067811865476))
    density = jnp.exp(-0.5 * pre_act * pre_act) * 0.3989422804014327
    return (pre_act * cumulative, cumulative + pre_act * density)


def remote(src, dst, send, recv, g, r):
    return pltpu.make_async_remote_copy(
        src_ref=src, dst_ref=dst, send_sem=send, recv_sem=recv,
        device_id=(g, r), device_id_type=MESH,
    )


def enter(outer, inner):
    g, r = lax.axis_index("g"), lax.axis_index("r")
    bar = pltpu.get_barrier_semaphore()
    for j in range(1, inner):
        pl.semaphore_signal(bar, inc=1, device_id=(g, r ^ j), device_id_type=MESH)
    for k in range(1, outer):
        pl.semaphore_signal(
            bar, inc=1, device_id=(lax.rem(g + k, outer), r), device_id_type=MESH
        )
    pl.semaphore_wait(bar, inner + outer - 2)
    return g, r


class PlaneSwap:
    def __init__(self, inner, g, r, src, dst, send, recv):
        self.copies = [
            remote(src(r ^ j), dst(r), send.at[j], recv.at[j], g, r ^ j) for j in range(1, inner)
        ]
        self.landed = [
            remote(dst(r ^ j), dst(r ^ j), send.at[j], recv.at[j], g, r ^ j)
            for j in range(1, inner)
        ]

    def start(self):
        for copy in self.copies:
            copy.start()

    def arrive(self):
        for copy in self.landed:
            copy.wait_recv()

    def sent(self):
        for copy in self.copies:
            copy.wait_send()


def near(outer, g, other):
    if outer != 4:
        return g != other
    return (g != other) & (jnp.abs(g - other) <= 2)


class ColumnGather:
    def __init__(self, outer, g, r, own, full, send, recv):
        self.outer, self.g, self.r = outer, g, r
        self.own, self.full, self.send, self.recv = own, full, send, recv

    def copy(self, dst):
        return remote(
            self.own, self.full.at[self.g], self.send.at[dst], self.recv.at[self.g], dst, self.r
        )

    def onward(self, src, dst):
        return remote(
            self.full.at[src], self.full.at[src], self.send.at[self.outer],
            self.recv.at[src], dst, self.r,
        )

    def start(self):
        order = range(self.outer)
        for dst in order:
            @pl.when(near(self.outer, self.g, dst))
            def _(dst=dst):
                self.copy(dst).start()

    def forward(self):
        if self.outer != 4:
            return
        for via, src, dst in ((2, 0, 3), (1, 3, 0)):
            @pl.when(self.g == via)
            def _(src=src, dst=dst):
                self.onward(src, dst).wait_recv()
                self.onward(src, dst).start()

    def arrive(self):
        for src in range(self.outer):
            waits = self.g != src
            if self.outer == 4 and src in (0, 3):
                waits = waits & (self.g != (2 if src == 0 else 1))
            @pl.when(waits)
            def _(src=src):
                self.onward(src, src).wait_recv()

    def sent(self):
        for dst in range(self.outer):
            @pl.when(near(self.outer, self.g, dst))
            def _(dst=dst):
                self.copy(dst).wait_send()
        if self.outer == 4:
            for via, src, dst in ((2, 0, 3), (1, 3, 0)):
                @pl.when(self.g == via)
                def _(src=src, dst=dst):
                    self.onward(src, dst).wait_send()


class ColumnSum:
    def __init__(self, outer, g, r, part, landing, send, recv):
        self.outer, self.g, self.r = outer, g, r
        self.part, self.landing, self.send, self.recv = part, landing, send, recv

    def copy(self, dst):
        return remote(
            self.part.at[dst], self.landing.at[self.g], self.send.at[dst],
            self.recv.at[self.g], dst, self.r,
        )

    def detour(self, dst, via):
        return remote(
            self.part.at[dst], self.landing.at[self.outer], self.send.at[dst],
            self.recv.at[self.outer], via, self.r,
        )

    def landed(self, slot):
        at = self.landing.at[slot]
        return remote(at, at, self.send.at[0], self.recv.at[slot], self.g, self.r)

    HOPS = ((0, 1, 3), (3, 2, 0))

    def start(self):
        if self.outer == 4:
            for src, via, dst in self.HOPS:
                @pl.when(self.g == src)
                def _(via=via, dst=dst):
                    self.detour(dst, via).start()
        for dst in range(self.outer):
            now = near(self.outer, self.g, dst)
            if self.outer == 4 and dst in (0, 3):
                now = now & (self.g != (1 if dst == 3 else 2))
            @pl.when(now)
            def _(dst=dst):
                self.copy(dst).start()

    def middle(self):
        if self.outer != 4:
            return
        for src, via, dst in self.HOPS:
            @pl.when(self.g == via)
            def _(dst=dst):
                self.landed(self.outer).wait_recv()
                both = self.part[dst].astype(F32) + self.landing[self.outer].astype(F32)
                self.landing[self.outer] = both.astype(self.landing.dtype)
                at = self.landing.at
                remote(
                    at[self.outer], at[self.g], self.send.at[dst], self.recv.at[self.g],
                    dst, self.r,
                ).start()

    def total(self, out):
        out[...] = self.part[self.g].astype(F32)
        for src in range(self.outer):
            @pl.when(near(self.outer, self.g, src))
            def _(src=src):
                self.landed(src).wait_recv()
                out[...] += self.landing[src].astype(F32)

    def sent(self):
        for dst in range(self.outer):
            @pl.when(self.g != dst)
            def _(dst=dst):
                self.copy(dst).wait_send()


class PlaneSum:
    def __init__(self, inner, g, r, part, beside, mixed, landing, send, recv):
        self.chips, self.g, self.r = inner // 2, g, r
        self.part, self.beside, self.mixed, self.landing = part, beside, mixed, landing
        self.send, self.recv = send, recv

    def across(self, j):
        twin = self.r ^ 1
        return remote(
            self.part.at[twin ^ (2 * j)], self.beside.at[j], self.send.at[j],
            self.recv.at[j], self.g, twin,
        )

    def out(self, j):
        n = self.chips
        return remote(
            self.mixed.at[j], self.landing.at[j], self.send.at[n + j], self.recv.at[n + j],
            self.g, self.r ^ (2 * j),
        )

    def start(self):
        for j in range(self.chips - 1, -1, -1):
            self.across(j).start()

    def middle(self):
        for j in range(self.chips - 1, 0, -1):
            self.across(j).wait_recv()
            both = self.part[self.r ^ (2 * j)].astype(F32) + self.beside[j].astype(F32)
            self.mixed[j] = both.astype(BF)
            self.out(j).start()
        self.across(0).wait_recv()

    def total(self, out):
        out[...] = self.part[self.r].astype(F32) + self.beside[0].astype(F32)
        for j in range(1, self.chips):
            self.out(j).wait_recv()
            out[...] += self.landing[j].astype(F32)

    def sent(self):
        for j in range(self.chips):
            self.across(j).wait_send()
        for j in range(1, self.chips):
            self.out(j).wait_send()


NN = (((1,), (0,)), ((), ()))
NT = (((1,), (1,)), ((), ()))
TN = (((0,), (0,)), ((), ()))
SLOT = 16


def dot(left, right, dims):
    return lax.dot_general(left, right, dims, preferred_element_type=F32)


def column_sum(values):
    return jnp.sum(values, axis=0, keepdims=True)


def layer_kernel(
    outer, inner, neat,
    x, cot, pos, vec, wq, wi, wd, wo,
    RES, GIN, GQ, GI, go_f, gd_f, TS, TSUM,
    X, C, POS, VEC, WQ, WD, WDZ, WI, WO, pq, pi, vecs, bq, bi, place,
    la, LM, GN, gq_w, gd_w,
    q, gc, kk, vv, gq, gk, gv, ctx, gb, cosine, lower, upper, back, away,
    act, gp, out_p, gn_p, out_b, out_m, out_l, gn_b, gn_m, gn_l,
    gi_w, go_w, gi_l, go_l, gq_l, gd_l, gd_z, gq_t, gi_t, gq_s, gi_s, gq_e, gi_e,
    table, table_z, total,
    loc, tok_s, tok_r, swap_s, swap_r, col_s, col_r, wd_s, wd_r, halo_s, halo_r,
    pl_s, pl_r, sum_s, sum_r, gd_ss, gd_rs,
):
    g, r = enter(outer, inner)
    tok_rows, width = x.shape
    rows, share = q.shape
    count = outer * inner
    part_rows = wd.shape[0]
    hidden = bi.shape[1]
    block = BLOCK
    span = block + REACH
    chunks = rows // block
    tail = REACH // block
    half = ROT // 2
    heads = share // HD
    twin, by_a, by_b, diag = r ^ 1, r ^ 2, r ^ 4, r ^ 6

    if neat:
        for n in range(3):
            for p in range(inner):
                at = (n * inner + p) * share
                pq[p, :, n * share : (n + 1) * share] = wq[:, at : at + share]
        piece_q = pq
    else:
        piece_q = wq
    swap_q = PlaneSwap(
        inner, g, r, lambda p: piece_q.at[p], lambda o: WQ.at[g, o], swap_s.at[0], swap_r.at[0]
    )
    swap_v = PlaneSwap(
        inner, g, r, lambda p: vec, lambda o: VEC.at[g, o], swap_s.at[1], swap_r.at[1]
    )
    swap_p = PlaneSwap(
        inner, g, r, lambda p: pos, lambda o: POS.at[o], swap_s.at[2], swap_r.at[2]
    )
    swap_v.start()
    swap_q.start()
    col_d = ColumnGather(outer, g, r, wd, WDZ, col_s.at[0], col_r.at[0])
    col_q = ColumnGather(outer, g, r, WQ.at[g], WQ, col_s.at[1], col_r.at[1])
    col_v = ColumnGather(outer, g, r, VEC.at[g], VEC, col_s.at[2], col_r.at[2])
    col_o = ColumnGather(outer, g, r, wo, WO, col_s.at[3], col_r.at[3])
    col_i = ColumnGather(outer, g, r, WI.at[g], WI, col_s.at[4], col_r.at[4])
    col_d.start()

    def slot(array, owner):
        return array.at[pl.ds(pl.multiple_of(owner * tok_rows, 16), tok_rows)]

    def tok(i, src, dst, to):
        return remote(src, dst, tok_s.at[i], tok_r.at[i], g, to)

    first_out = [
        tok(0, x, slot(X, r), by_a), tok(1, cot, slot(C, r), by_b),
        tok(2, cot, slot(C, r), by_a), tok(3, x, slot(X, r), by_b),
    ]
    for copy in first_out:
        copy.start()
    pair = [tok(6, x, slot(X, r), twin), tok(7, cot, slot(C, r), twin)]
    for copy in pair:
        copy.start()
    swap_p.start()
    own = [
        (x, slot(X, r)), (cot, slot(C, r)), (piece_q.at[r], WQ.at[g, r]), (vec, VEC.at[g, r]),
        (pos, POS.at[r]), (wd, WDZ.at[g]), (wo, WO.at[g]),
    ]
    own = [pltpu.make_async_copy(a, b, loc.at[i]) for i, (a, b) in enumerate(own)]
    for copy in own:
        copy.start()
    for copy in own:
        copy.wait()
    swap_v.arrive()
    col_v.start()
    swap_q.arrive()
    col_q.start()
    if neat:
        for n in range(outer):
            for p in range(inner):
                at = (n * inner + p) * 128
                pi[p, :, n * 128 : (n + 1) * 128] = wi[:, at : at + 128]
        piece_i = pi
    else:
        piece_i = wi
    swap_i = PlaneSwap(
        inner, g, r, lambda p: piece_i.at[p], lambda o: WI.at[g, o], swap_s.at[3], swap_r.at[3]
    )
    mine_i = pltpu.make_async_copy(piece_i.at[r], WI.at[g, r], loc.at[7])
    mine_i.start()

    def pass_on(index, array, owner):
        copy = tok(index, slot(array, owner), slot(array, owner), twin)
        copy.start()
        pair.append(copy)

    def landed(index, array, owner):
        tok(index, slot(array, owner), slot(array, owner), twin).wait_recv()

    col_d.forward()
    col_v.forward()
    col_v.arrive()
    lines = width // 128
    shift = lines.bit_length() - 1
    kinds = 6 * lines
    want = (kinds + 3 + 7) // 8 * 8
    o = lax.broadcasted_iota(jnp.int32, (want, count * SLOT), 0)
    c = lax.broadcasted_iota(jnp.int32, (want, count * SLOT), 1)
    d, n = c >> 4, c & 15
    line = (d * part_rows) >> 7
    plain = (o < kinds) & (n == (o >> shift)) & (line == (o & (lines - 1)))
    line_q = (d * (3 * part_rows)) >> 7
    goal = (o - kinds) * lines + r
    third = (o >= kinds) & (o < kinds + 3)
    third = third & (((n == 6) & (line_q == goal)) | ((n == 7) & (line_q + 1 == goal)))
    pick = jnp.where(plain | third, 1.0, 0.0).astype(BF)
    found = dot(pick, VEC[...].reshape(count * SLOT, 128), NN)

    def vector(k):
        return jnp.concatenate(
            [found[k * lines + j : k * lines + j + 1, :] for j in range(lines)], axis=1
        )

    for k in range(4):
        vecs[k : k + 1, :] = vector(k)
    vecs[4:5, :] = vector(4) + vector(5)
    bq[0:1, :] = jnp.concatenate([found[kinds + t : kinds + t + 1, :] for t in range(3)], axis=1)
    unit = hidden // outer
    bi[0:1, :] = jnp.concatenate(
        [VEC[z, r][8:9, :unit].astype(F32) for z in range(outer)], axis=1
    )

    def prepare(owner):
        at = pl.ds(pl.multiple_of(owner * tok_rows, 16), tok_rows)
        normed, _ = norm_stats(X[at, :])
        la[at, :] = (normed * vecs[0:1, :] + vecs[1:2, :]).astype(BF)
        LM[at, :] = (normed * vecs[2:3, :] + vecs[3:4, :]).astype(BF)

    landed(0, X, by_a)
    onward_a = tok(4, slot(X, by_a), slot(X, by_a), by_b)
    onward_a.start()
    pass_on(8, X, by_a)
    landed(1, C, by_b)
    onward_b = tok(5, slot(C, by_b), slot(C, by_b), by_a)
    onward_b.start()
    pass_on(9, C, by_b)
    swap_i.start()
    prepare(r)
    landed(6, X, twin)
    prepare(twin)
    col_d.arrive()
    for z in range(outer):
        owner = z * inner + r
        to, at = owner // outer, lax.rem(owner, outer)

        @pl.when(to == r)
        def _():
            WD[at] = WDZ[z]

        @pl.when(to != r)
        def _():
            remote(WDZ.at[z], WD.at[at], wd_s.at[z], wd_r.at[at], g, to).start()

    prepare(by_a)
    landed(2, C, by_a)
    pass_on(10, C, by_a)
    landed(3, X, by_b)
    pass_on(11, X, by_b)
    col_q.forward()
    col_o.start()
    prepare(by_b)
    landed(8, X, twin ^ 2)
    prepare(twin ^ 2)
    swap_p.arrive()
    lane_parts = []
    for p in range(inner):
        held = POS[p].astype(F32)
        for k in range(0, tok_rows, 128):
            lane_parts.append(held[k // 128 : k // 128 + 1, : min(128, tok_rows - k)])
    place[0:1, :] = jnp.concatenate(lane_parts, axis=1)
    step_of = lax.broadcasted_iota(jnp.int32, (half, rows), 0).astype(F32)
    angles = place[0:1, :] * jnp.exp(step_of * (-2.0 / ROT * jnp.log(ROPE_BASE)))
    cos_t, sin_t = jnp.cos(angles), jnp.sin(angles)
    blank = jnp.zeros((half, rows), F32)
    quiet = jnp.zeros((HD - ROT, rows), F32)
    tall = lambda parts: jnp.transpose(jnp.concatenate(parts * heads, axis=0))
    cosine[...] = tall([cos_t, cos_t, quiet + 1.0])
    lower[...] = tall([-sin_t, blank, quiet])
    upper[...] = tall([blank, sin_t, quiet])
    landed(4, X, diag)
    pass_on(12, X, diag)
    landed(5, C, diag)
    pass_on(13, C, diag)
    landed(11, X, twin ^ 4)
    prepare(twin ^ 4)
    prepare(diag)
    landed(12, X, twin ^ 6)
    prepare(twin ^ 6)
    for i, owner in ((7, twin), (9, twin ^ 4), (10, twin ^ 2), (13, twin ^ 6)):
        landed(i, C, owner)
    for z in range(outer):
        source = lax.rem(r * outer + z, inner)

        @pl.when(source != r)
        def _():
            remote(WD.at[z], WD.at[z], wd_s.at[z], wd_r.at[z], g, source).wait_recv()

    col_q.arrive()
    mine_i.wait()
    swap_i.arrive()
    col_i.start()

    def turn(values, at, orient):
        ahead_v = pltpu.roll(values, share - half, 1)
        behind_v = pltpu.roll(values, half, 1)
        return values * cosine[at, :] + orient * (ahead_v * lower[at, :] + behind_v * upper[at, :])

    def chunk(i):
        return pl.ds(pl.multiple_of(i * block, block), block)

    def ahead(i):
        return pl.ds(pl.multiple_of(i * block + REACH, block), block)

    w_qkv = lambda: WQ[...].reshape(width, 3 * share)
    w_dense = lambda: WD[...].reshape(share, width)

    def project(j, carry):
        i = chunks - 1 - j
        at = chunk(i)
        mixed = dot(la[at, :], w_qkv(), NN) + bq[0:1, :]
        q[at, :] = turn(mixed[:, :share], at, 1.0).astype(BF)
        kk[ahead(i), :] = turn(mixed[:, share : 2 * share], at, 1.0).astype(BF)
        vv[ahead(i), :] = mixed[:, 2 * share :].astype(BF)
        gc[at, :] = dot(C[at, :], w_dense(), NT).astype(BF)
        return carry

    first, last = pl.ds(0, REACH), pl.ds(rows, REACH)

    def halo(n, src, dst, to):
        return remote(src, dst, halo_s.at[n], halo_r.at[n], to, r)

    lax.fori_loop(0, tail, project, 0)

    @pl.when(g < outer - 1)
    def _():
        halo(0, kk.at[last], kk.at[first], g + 1).start()
        halo(1, vv.at[last], vv.at[first], g + 1).start()

    @pl.when(g == 0)
    def _():
        kk[first, :] = jnp.zeros((REACH, share), BF)
        vv[first, :] = jnp.zeros((REACH, share), BF)

    lax.fori_loop(tail, chunks, project, 0)
    gk[...] = jnp.zeros_like(gk)
    gv[...] = jnp.zeros_like(gv)

    def attend(i, carry):
        at = chunk(i)
        keys = pl.ds(pl.multiple_of(i * block, block), span)
        reach = place[0:1, at].astype(jnp.int32)
        spread = (
            lax.broadcasted_iota(jnp.int32, (span, block), 1) + REACH
            - lax.broadcasted_iota(jnp.int32, (span, block), 0)
        )
        allowed = (spread >= 0) & (spread <= reach)
        ctx_h, gq_h, gk_h, gv_h = [], [], [], []
        for h in range(heads):
            lanes = slice(h * HD, (h + 1) * HD)
            q_h, gc_h = q[at, lanes], gc[at, lanes]
            k_h, v_h = kk[keys, lanes], vv[keys, lanes]
            scores = jnp.where(allowed, dot(k_h, q_h, NT) * HD ** (-0.5), -1e30)
            top = jnp.max(scores, axis=0, keepdims=True)
            weight = jnp.exp(scores - top)
            probs = weight * (1.0 / jnp.sum(weight, axis=0, keepdims=True))
            probs_b = probs.astype(BF)
            ctx_h.append(dot(probs_b, v_h, TN))
            grad_probs = dot(v_h, gc_h, NT)
            row_dot = jnp.sum(probs * grad_probs, axis=0, keepdims=True)
            grad_s = (probs * (grad_probs - row_dot) * HD ** (-0.5)).astype(BF)
            gq_h.append(dot(grad_s, k_h, TN))
            gk_h.append(dot(grad_s, q_h, NN))
            gv_h.append(dot(probs_b, gc_h, NN))
        ctx[at, :] = jnp.concatenate(ctx_h, axis=1).astype(BF)
        gq[at, :] = jnp.concatenate(gq_h, axis=1)
        gk[keys, :] += jnp.concatenate(gk_h, axis=1)
        gv[keys, :] += jnp.concatenate(gv_h, axis=1)
        return carry

    lax.fori_loop(tail, chunks, attend, 0)
    col_o.forward()

    @pl.when(g > 0)
    def _():
        halo(0, kk.at[first], kk.at[first], g).wait_recv()
        halo(1, vv.at[first], vv.at[first], g).wait_recv()

    lax.fori_loop(0, tail, attend, 0)
    away[0] = gk[first, :].astype(BF)
    away[1] = gv[first, :].astype(BF)

    @pl.when(g > 0)
    def _():
        halo(2, away, back, g - 1).start()

    @pl.when(g == outer - 1)
    def _():
        back[...] = jnp.zeros_like(back)

    table[...] = jnp.zeros_like(table)

    def finish(i, carry):
        at = chunk(i)
        grads = jnp.concatenate(
            [
                turn(gq[at, :], at, -1.0), turn(gk[ahead(i), :], at, -1.0),
                gv[ahead(i), :],
            ],
            axis=1,
        )
        table[5:6, : 3 * share] += column_sum(grads)
        grads_b = grads.astype(BF)
        gb[at, :] = grads_b
        grad_left = dot(grads_b, w_qkv(), NT)
        normed, _ = norm_stats(X[at, :])
        table[0:1, :] += column_sum(grad_left * normed)
        table[1:2, :] += column_sum(grad_left)
        GN[at, :] = (grad_left * vecs[0:1, :]).astype(BF)
        return carry

    lax.fori_loop(0, chunks - tail, finish, 0)
    col_i.forward()

    @pl.when(g < outer - 1)
    def _():
        halo(2, away, back, g).wait_recv()

    gk[last, :] += back[0].astype(F32)
    gv[last, :] += back[1].astype(F32)
    lax.fori_loop(chunks - tail, chunks, finish, 0)

    sum_q = ColumnSum(outer, g, r, gq_w, gq_l, sum_s.at[0], sum_r.at[0])
    sum_i = ColumnSum(outer, g, r, gi_w, gi_l, sum_s.at[1], sum_r.at[1])
    sum_o = ColumnSum(outer, g, r, go_w, go_l, sum_s.at[2], sum_r.at[2])
    sum_d = ColumnSum(outer, g, r, gd_z, gd_l, sum_s.at[3], sum_r.at[3])
    part = inner * part_rows
    for t in range(outer):
        grad = dot(la[:, t * part : (t + 1) * part], gb[...], TN).astype(BF)
        gq_w[t] = grad.reshape(gq_w.shape[1:])
    sum_q.start()
    lanes_d = min(width, 256)
    for t in range(width // lanes_d):
        at = slice(t * lanes_d, (t + 1) * lanes_d)
        grad = dot(ctx[...], C[:, at], TN).astype(BF)
        gd_w[:, :, at] = grad.reshape(outer, part_rows, lanes_d)
    for i in range(outer):
        owner = r * outer + i
        z, to = owner // inner, lax.rem(owner, inner)

        @pl.when(to == r)
        def _():
            gd_z[z] = gd_w[i]

        @pl.when(to != r)
        def _():
            remote(gd_w.at[i], gd_z.at[z], gd_ss.at[i], gd_rs.at[z], g, to).start()

    col_o.arrive()
    col_i.arrive()
    w_in = lambda: WI[...].reshape(width, hidden)
    w_out = lambda: WO[...].reshape(hidden, width)

    def inside(i, carry):
        at = chunk(i)
        pre_act = dot(LM[at, :], w_in(), NN) + bi[0:1, :]
        activated, slope = gelu_pair(pre_act)
        act[at, :] = activated.astype(BF)
        grad_pre = dot(C[at, :], w_out(), NT) * slope
        gp[at, :] = grad_pre.astype(BF)
        table[6:7, :hidden] += column_sum(grad_pre)
        return carry

    lax.fori_loop(0, chunks, inside, 0)
    for t in range(outer):
        go_w[t] = dot(act[:, t * unit : (t + 1) * unit], C[...], TN).astype(BF)
    sum_o.start()
    for t in range(outer):
        grad = dot(LM[:, t * part : (t + 1) * part], gp[...], TN).astype(BF)
        gi_w[t] = grad.reshape(gi_w.shape[1:])
    sum_i.start()
    for z in range(outer):
        source = (z * inner + r) // outer

        @pl.when(source != r)
        def _():
            remote(gd_z.at[z], gd_z.at[z], gd_ss.at[z], gd_rs.at[z], g, source).wait_recv()

    sum_d.start()

    def outside(i, carry):
        at = pl.ds(pl.multiple_of(i * tok_rows, 16), tok_rows)
        mlp_out = dot(act[at, :], w_out(), NN)
        out_p[i] = (dot(ctx[at, :], w_dense(), NN) + mlp_out).astype(BF)
        grad_left = dot(gp[at, :], w_in(), NT)
        normed, _ = norm_stats(X[at, :])
        table[2:3, :] += column_sum(grad_left * normed)
        table[3:4, :] += column_sum(grad_left)
        gn_p[i] = (GN[at, :].astype(F32) + grad_left * vecs[2:3, :]).astype(BF)
        return carry

    lax.fori_loop(0, inner, outside, 0)
    plane_o = PlaneSum(inner, g, r, out_p, out_b, out_m, out_l, pl_s.at[0], pl_r.at[0])
    plane_n = PlaneSum(inner, g, r, gn_p, gn_b, gn_m, gn_l, pl_s.at[1], pl_r.at[1])
    plane_n.start()
    plane_o.start()
    top_f = cot[...].astype(F32)
    table[4:5, :] = column_sum(top_f)
    col_t = ColumnGather(outer, g, r, table, table_z, col_s.at[5], col_r.at[5])
    col_t.start()
    sum_q.middle()
    sum_o.middle()
    plane_n.middle()
    plane_o.middle()
    sum_d.middle()
    sum_i.middle()
    col_t.forward()
    sum_q.total(gq_t)
    gq_s[...] = gq_t[...].astype(BF)
    swap_gq = PlaneSwap(
        inner, g, r, lambda p: gq_s.at[p], lambda o: gq_e.at[o], swap_s.at[4], swap_r.at[4]
    )
    swap_gq.start()
    gq_e[r] = gq_s[r]
    col_t.arrive()
    table_z[g] = table[...]
    TS[r] = jnp.sum(table_z[...], axis=0)
    swap_t = PlaneSwap(
        inner, g, r, lambda p: TS.at[r], lambda o: TS.at[o], swap_s.at[5], swap_r.at[5]
    )
    swap_t.start()
    plane_o.total(total)
    x_f = x[...].astype(F32)
    RES[...] = (x_f + total[...] + vecs[4:5, :]).astype(BF)
    plane_n.total(total)
    own_normed, inv_scale = norm_stats(x[...])
    grad_normed = total[...]
    GIN[...] = top_f + inv_scale * (
        grad_normed
        - jnp.mean(grad_normed, axis=-1, keepdims=True)
        - own_normed * jnp.mean(grad_normed * own_normed, axis=-1, keepdims=True)
    )
    sum_o.total(go_f)
    sum_d.total(gd_f)
    sum_i.total(gi_t)
    gi_s[...] = gi_t[...].astype(BF)
    swap_gi = PlaneSwap(
        inner, g, r, lambda p: gi_s.at[p], lambda o: gi_e.at[o], swap_s.at[6], swap_r.at[6]
    )
    swap_gi.start()
    gi_e[r] = gi_s[r]

    def settle(out, arrived):
        if not neat:
            out[...] = arrived[...]
            return
        for owner in range(inner):
            for n in range(arrived.shape[2] // 128):
                at = (n * inner + owner) * 128
                out[:, at : at + 128] = arrived[owner][:, n * 128 : n * 128 + 128].astype(F32)

    swap_gq.arrive()
    settle(GQ, gq_e)
    swap_t.arrive()
    TSUM[...] = jnp.sum(TS[...], axis=0)
    swap_gi.arrive()
    settle(GI, gi_e)
    for copy in first_out + pair + [onward_a, onward_b]:
        copy.wait_send()
    for i in range(outer):
        to = (i * inner + r) // outer

        @pl.when(to != r)
        def _():
            remote(WDZ.at[i], WD.at[i], wd_s.at[i], wd_r.at[i], g, to).wait_send()

        to = lax.rem(r * outer + i, inner)

        @pl.when(to != r)
        def _():
            remote(gd_w.at[i], gd_z.at[i], gd_ss.at[i], gd_rs.at[i], g, to).wait_send()

    @pl.when(g < outer - 1)
    def _():
        halo(0, kk.at[last], kk.at[first], g).wait_send()
        halo(1, vv.at[last], vv.at[first], g).wait_send()

    @pl.when(g > 0)
    def _():
        halo(2, away, back, g).wait_send()

    for item in (
        swap_q, swap_v, swap_p, swap_i, col_d, col_q, col_v, col_o, col_i, plane_o, plane_n,
        sum_q, sum_i, sum_o, sum_d, col_t, swap_gq, swap_gi, swap_t,
    ):
        item.sent()


def layer(outer, inner, x, cot, pos, vec, wq, wi, wd, wo):
    shape = jax.ShapeDtypeStruct
    dma = pltpu.SemaphoreType.DMA
    vmem = pl.BlockSpec(memory_space=pltpu.VMEM)
    tok_rows, width = x.shape
    part_rows, unit = wd.shape[0], wo.shape[0]
    rows = inner * tok_rows
    share = width // inner
    hidden = outer * unit
    neat = whole_tiles(unit, share, part_rows)
    chips = inner // 2
    v = pltpu.VMEM
    piece_q = (inner, part_rows, 3 * share)
    piece_i = (inner, part_rows, hidden)
    piece_o = (unit, width)
    piece_d = (part_rows, width)
    outs = (
        shape((tok_rows, width), BF), shape((tok_rows, width), F32),
        shape((part_rows, 3 * width), F32) if neat else shape(piece_q, BF),
        shape((part_rows, hidden * inner), F32) if neat else shape(piece_i, BF),
        shape(piece_o, F32), shape(piece_d, F32), shape((inner, 8, width), F32),
        shape((8, width), F32),
    )
    wide = v((rows, width), BF)
    own = (rows, share)
    more = (rows + REACH, share)
    quad = v((chips, tok_rows, width), BF)
    group = v((inner, tok_rows, width), BF)
    scratch = [
        wide, wide, v((inner, *pos.shape), jnp.int32), v((outer, inner, *vec.shape), BF),
        v((outer, *piece_q), BF), v((outer, *piece_d), BF), v((outer, *piece_d), BF),
        v((outer, *piece_i), BF), v((outer, *piece_o), BF), v(piece_q, BF), v(piece_i, BF),
        v((8, width), F32), v((8, 3 * share), F32), v((8, hidden), F32), v((8, rows), F32),
        wide, wide, wide, v((outer, *piece_q), BF), v((outer, *piece_d), BF),
        v(own, BF), v(own, BF), v(more, BF), v(more, BF), v(own, F32), v(more, F32),
        v(more, F32), v(own, BF), v((rows, 3 * share), BF), v(own, F32), v(own, F32),
        v(own, F32), v((2, REACH, share), BF), v((2, REACH, share), BF),
        v((rows, hidden), BF), v((rows, hidden), BF), group, group, *([quad] * 6),
        v((outer, *piece_i), BF), v((outer, *piece_o), BF),
        v((outer + 1, *piece_i), BF), v((outer + 1, *piece_o), BF),
        v((outer + 1, *piece_q), BF), v((outer + 1, *piece_d), BF), v((outer, *piece_d), BF),
        v(piece_q, F32), v(piece_i, F32), v(piece_q, BF), v(piece_i, BF),
        v(piece_q, BF), v(piece_i, BF), v((8, width), F32), v((outer, 8, width), F32),
        v((tok_rows, width), F32),
        dma((8,)), dma((14,)), dma((14,)), dma((7, inner)), dma((7, inner)),
        dma((6, outer + 1)), dma((6, outer + 1)), dma((outer,)), dma((outer,)),
        dma((3,)), dma((3,)), dma((2, 2 * chips)), dma((2, 2 * chips)),
        dma((4, outer + 1)), dma((4, outer + 1)), dma((outer,)), dma((outer,)),
    ]
    out = pl.pallas_call(
        functools.partial(layer_kernel, outer, inner, neat),
        out_shape=outs,
        in_specs=[vmem] * 8,
        out_specs=[vmem] * 8,
        scratch_shapes=scratch,
        compiler_params=pltpu.CompilerParams(
            collective_id=0, has_side_effects=True, vmem_limit_bytes=VMEM_LIMIT
        ),
    )(x, cot, pos, vec, wq, wi, wd, wo)
    out = list(out)
    if not neat:
        for n, parts in ((2, 3), (3, outer)):
            out[n] = (
                out[n].reshape(inner, part_rows, parts, -1)
                .transpose(1, 2, 0, 3)
                .reshape(part_rows, -1)
                .astype(F32)
            )
    return out


def whole_tiles(unit, share, part_rows):
    return unit == 128 and share == 128 and part_rows % 16 == 0


def body(
    layer_input,
    ln1_gain,
    ln1_bias,
    qkv_weight,
    qkv_bias,
    dense_weight,
    dense_bias,
    ln2_gain,
    ln2_bias,
    fc_in_weight,
    fc_in_bias,
    fc_out_weight,
    fc_out_bias,
    positions,
    cotangent,
):
    bf = jnp.bfloat16
    f32 = jnp.float32
    outer = lax.axis_size("g")
    inner = lax.axis_size("r")
    count = outer * inner
    rank = lax.axis_index("r")
    tok_rows, width = layer_input.shape
    part_rows = qkv_weight.shape[0]
    share = width // inner
    unit = fc_out_weight.shape[0]
    hidden = outer * unit
    rows = inner * tok_rows

    device = lax.axis_index("g") * inner + rank
    lane = jnp.arange(128, dtype=jnp.int32)
    mine = lane // part_rows == lax.rem(device, 128 // part_rows)
    vectors = [ln1_gain, ln1_bias, ln2_gain, ln2_bias, dense_bias, fc_out_bias]
    lines = [
        jnp.where(mine, jnp.tile(v.astype(f32), 128 // part_rows), 0.0)[None] for v in vectors
    ]
    size = qkv_bias.shape[0]
    start = lax.rem(device * size, 128)
    spread = lax.dynamic_update_slice(jnp.zeros((256,), f32), qkv_bias.astype(f32), (start,))
    lines.append(spread.reshape(2, 128))
    lines.append(jnp.pad(fc_in_bias.astype(f32)[None], ((0, 0), (0, 128 - unit))))
    lines.append(jnp.zeros((SLOT - 9, 128), f32))
    vec = jnp.concatenate(lines, axis=0).astype(bf)
    pos = jnp.pad(positions, (0, 1024 - tok_rows)).reshape(8, 128)
    wq, wi = qkv_weight, fc_in_weight
    if not whole_tiles(unit, share, part_rows):
        wq = (
            wq.reshape(part_rows, 3, inner, share)
            .transpose(2, 0, 1, 3)
            .reshape(inner, part_rows, 3 * share)
        )
        wi = (
            wi.reshape(part_rows, outer, inner, unit)
            .transpose(2, 0, 1, 3)
            .reshape(inner, part_rows, hidden)
        )
    result, grad_in, g_qkv_w, g_in_w, g_out_w, g_dense_w, table, sums = layer(
        outer, inner, layer_input, cotangent, pos, vec, wq, wi, dense_weight, fc_out_weight
    )
    own = lax.dynamic_slice_in_dim(sums, device * part_rows, part_rows, axis=1)
    out = [own[n] for n in range(5)]
    for n, lanes, parts in ((5, 3 * share, 3), (6, hidden, outer)):
        vector = table[:, n, :lanes].reshape(inner, parts, -1).transpose(1, 0, 2).reshape(-1)
        size = vector.shape[0] // count
        out.append(lax.dynamic_slice_in_dim(vector, device * size, size))
    return (
        result,
        grad_in,
        out[0],
        out[1],
        g_qkv_w,
        out[5],
        g_dense_w,
        out[4],
        out[2],
        out[3],
        g_in_w,
        out[6],
        g_out_w,
        out[4],
    )


def solution(mesh):
    inner = GROUP
    split = Mesh(mesh.devices.reshape(-1, inner), ("g", "r"))
    flat = P(("g", "r"))
    tall = P(("g", "r"), None)
    in_specs = (
        tall, flat, flat, tall, flat, tall, flat, flat, flat, tall, flat, tall, flat, flat, tall,
    )
    out_specs = (
        tall, tall, flat, flat, tall, flat, tall, flat, flat, flat, tall, flat, tall, flat,
    )
    return jax.shard_map(body, mesh=split, in_specs=in_specs, out_specs=out_specs, check_vma=False)
```

```python
import functools

import jax
import jax.numpy as jnp
from jax import lax
from jax.experimental import pallas as pl
from jax.experimental.pallas import tpu as pltpu
from jax.sharding import Mesh
from jax.sharding import PartitionSpec as P

HEADS = 16
HD = 64
ROT = 16
REACH = 512
GROUP = 8
BLOCK = 256
EPSILON = 1e-05
ROPE_BASE = 10000.0
MESH = pl.DeviceIdType.MESH
BF = jnp.bfloat16
F32 = jnp.float32
VMEM_LIMIT = 60 * 2**20


def norm_stats(inputs):
    values_f = inputs.astype(jnp.float32)
    centre = jnp.mean(values_f, axis=-1, keepdims=True)
    shifted = values_f - centre
    variance = jnp.mean(shifted * shifted, axis=-1, keepdims=True)
    inv_scale = lax.rsqrt(variance + EPSILON)
    return (shifted * inv_scale, inv_scale)


def gelu_pair(pre_act):
    cumulative = 0.5 * (1.0 + lax.erf(pre_act * 0.7071067811865476))
    density = jnp.exp(-0.5 * pre_act * pre_act) * 0.3989422804014327
    return (pre_act * cumulative, cumulative + pre_act * density)


def remote(src, dst, send, recv, g, r):
    return pltpu.make_async_remote_copy(
        src_ref=src, dst_ref=dst, send_sem=send, recv_sem=recv,
        device_id=(g, r), device_id_type=MESH,
    )


def enter(outer, inner):
    g, r = lax.axis_index("g"), lax.axis_index("r")
    bar = pltpu.get_barrier_semaphore()
    for j in range(1, inner):
        pl.semaphore_signal(bar, inc=1, device_id=(g, r ^ j), device_id_type=MESH)
    for k in range(1, outer):
        pl.semaphore_signal(
            bar, inc=1, device_id=(lax.rem(g + k, outer), r), device_id_type=MESH
        )
    pl.semaphore_wait(bar, inner + outer - 2)
    return g, r


class PlaneSwap:
    def __init__(self, inner, g, r, src, dst, send, recv):
        self.copies = [
            remote(src(r ^ j), dst(r), send.at[j], recv.at[j], g, r ^ j) for j in range(1, inner)
        ]
        self.landed = [
            remote(dst(r ^ j), dst(r ^ j), send.at[j], recv.at[j], g, r ^ j)
            for j in range(1, inner)
        ]

    def start(self):
        for copy in self.copies:
            copy.start()

    def arrive(self):
        for copy in self.landed:
            copy.wait_recv()

    def sent(self):
        for copy in self.copies:
            copy.wait_send()


def near(outer, g, other):
    if outer != 4:
        return g != other
    return (g != other) & (jnp.abs(g - other) <= 2)


class ColumnGather:
    def __init__(self, outer, g, r, own, full, send, recv):
        self.outer, self.g, self.r = outer, g, r
        self.own, self.full, self.send, self.recv = own, full, send, recv

    def copy(self, dst):
        return remote(
            self.own, self.full.at[self.g], self.send.at[dst], self.recv.at[self.g], dst, self.r
        )

    def onward(self, src, dst):
        return remote(
            self.full.at[src], self.full.at[src], self.send.at[self.outer],
            self.recv.at[src], dst, self.r,
        )

    def start(self):
        order = range(self.outer)
        for dst in order:
            @pl.when(near(self.outer, self.g, dst))
            def _(dst=dst):
                self.copy(dst).start()

    def forward(self):
        if self.outer != 4:
            return
        for via, src, dst in ((2, 0, 3), (1, 3, 0)):
            @pl.when(self.g == via)
            def _(src=src, dst=dst):
                self.onward(src, dst).wait_recv()
                self.onward(src, dst).start()

    def arrive(self):
        for src in range(self.outer):
            waits = self.g != src
            if self.outer == 4 and src in (0, 3):
                waits = waits & (self.g != (2 if src == 0 else 1))
            @pl.when(waits)
            def _(src=src):
                self.onward(src, src).wait_recv()

    def sent(self):
        for dst in range(self.outer):
            @pl.when(near(self.outer, self.g, dst))
            def _(dst=dst):
                self.copy(dst).wait_send()
        if self.outer == 4:
            for via, src, dst in ((2, 0, 3), (1, 3, 0)):
                @pl.when(self.g == via)
                def _(src=src, dst=dst):
                    self.onward(src, dst).wait_send()


class ColumnSum:
    def __init__(self, outer, g, r, part, landing, send, recv):
        self.outer, self.g, self.r = outer, g, r
        self.part, self.landing, self.send, self.recv = part, landing, send, recv

    def copy(self, dst):
        return remote(
            self.part.at[dst], self.landing.at[self.g], self.send.at[dst],
            self.recv.at[self.g], dst, self.r,
        )

    def detour(self, dst, via):
        return remote(
            self.part.at[dst], self.landing.at[self.outer], self.send.at[dst],
            self.recv.at[self.outer], via, self.r,
        )

    def landed(self, slot):
        at = self.landing.at[slot]
        return remote(at, at, self.send.at[0], self.recv.at[slot], self.g, self.r)

    HOPS = ((0, 1, 3), (3, 2, 0))

    def start(self):
        if self.outer == 4:
            for src, via, dst in self.HOPS:
                @pl.when(self.g == src)
                def _(via=via, dst=dst):
                    self.detour(dst, via).start()
        for dst in range(self.outer):
            now = near(self.outer, self.g, dst)
            if self.outer == 4:
                now = now & (self.g != 0) & (self.g != 3)
                if dst in (0, 3):
                    now = now & (self.g != (1 if dst == 3 else 2))
            @pl.when(now)
            def _(dst=dst):
                self.copy(dst).start()

    def rest(self):
        if self.outer != 4:
            return
        for dst in (2, 1):
            @pl.when(self.g == 0)
            def _(dst=dst):
                self.copy(dst).start()

            @pl.when(self.g == 3)
            def _(dst=dst):
                self.copy(3 - dst).start()

    def middle(self):
        if self.outer != 4:
            return
        for src, via, dst in self.HOPS:
            @pl.when(self.g == via)
            def _(dst=dst):
                self.landed(self.outer).wait_recv()
                both = self.part[dst].astype(F32) + self.landing[self.outer].astype(F32)
                self.landing[self.outer] = both.astype(self.landing.dtype)
                at = self.landing.at
                remote(
                    at[self.outer], at[self.g], self.send.at[dst], self.recv.at[self.g],
                    dst, self.r,
                ).start()

    def total(self, out):
        out[...] = self.part[self.g].astype(F32)
        for src in range(self.outer):
            @pl.when(near(self.outer, self.g, src))
            def _(src=src):
                self.landed(src).wait_recv()
                out[...] += self.landing[src].astype(F32)

    def sent(self):
        for dst in range(self.outer):
            @pl.when(self.g != dst)
            def _(dst=dst):
                self.copy(dst).wait_send()


class PlaneSum:
    def __init__(self, inner, g, r, part, beside, mixed, landing, send, recv):
        self.chips, self.g, self.r = inner // 2, g, r
        self.part, self.beside, self.mixed, self.landing = part, beside, mixed, landing
        self.send, self.recv = send, recv

    def across(self, j):
        twin = self.r ^ 1
        return remote(
            self.part.at[twin ^ (2 * j)], self.beside.at[j], self.send.at[j],
            self.recv.at[j], self.g, twin,
        )

    def out(self, j):
        n = self.chips
        return remote(
            self.mixed.at[j], self.landing.at[j], self.send.at[n + j], self.recv.at[n + j],
            self.g, self.r ^ (2 * j),
        )

    def start(self):
        for j in range(self.chips - 1, -1, -1):
            self.across(j).start()

    def middle(self):
        for j in range(self.chips - 1, 0, -1):
            self.across(j).wait_recv()
            both = self.part[self.r ^ (2 * j)].astype(F32) + self.beside[j].astype(F32)
            self.mixed[j] = both.astype(BF)
            self.out(j).start()
        self.across(0).wait_recv()

    def total(self, out):
        out[...] = self.part[self.r].astype(F32) + self.beside[0].astype(F32)
        for j in range(1, self.chips):
            self.out(j).wait_recv()
            out[...] += self.landing[j].astype(F32)

    def sent(self):
        for j in range(self.chips):
            self.across(j).wait_send()
        for j in range(1, self.chips):
            self.out(j).wait_send()


NN = (((1,), (0,)), ((), ()))
NT = (((1,), (1,)), ((), ()))
TN = (((0,), (0,)), ((), ()))
SLOT = 16


def dot(left, right, dims):
    return lax.dot_general(left, right, dims, preferred_element_type=F32)


def column_sum(values):
    return jnp.sum(values, axis=0, keepdims=True)


def layer_kernel(
    outer, inner, neat,
    x, cot, pos_in, v0, v1, v2, v3, v4, v5, bq_in, bi_in, wq, wi, wd, wo,
    RES, GIN, GQ, GI, go_f, gd_f, TS, TSUM,
    X, C, POS, VEC, WQ, WD, WDZ, WI, WO, pq, pi, vecs, bq, bi, place,
    la, LM, GN, gq_w, gd_w,
    q, gc, kk, vv, gq, gk, gv, ctx, gb, cosine, lower, upper, back, away,
    act, gp, out_p, gn_p, out_b, out_m, out_l, gn_b, gn_m, gn_l,
    gi_w, go_w, gi_l, go_l, gq_l, gd_l, gd_z, gq_t, gi_t, gq_s, gi_s, gq_e, gi_e,
    table, table_z, total, vec, pos,
    loc, tok_s, tok_r, swap_s, swap_r, col_s, col_r, wd_s, wd_r, halo_s, halo_r,
    pl_s, pl_r, sum_s, sum_r, gd_ss, gd_rs,
):
    g, r = enter(outer, inner)
    tok_rows, width = x.shape
    rows, share = q.shape
    count = outer * inner
    part_rows = wd.shape[0]
    hidden = bi.shape[1]
    block = BLOCK
    span = block + REACH
    chunks = rows // block
    tail = REACH // block
    half = ROT // 2
    heads = share // HD
    twin, by_a, by_b, diag = r ^ 1, r ^ 2, r ^ 4, r ^ 6

    device = g * inner + r

    def padded(ref, lanes):
        held = ref[...].astype(F32)
        if held.shape[1] == lanes:
            return held
        return jnp.concatenate([held, jnp.zeros((1, lanes - held.shape[1]), F32)], axis=1)

    blank_row = jnp.zeros((1, 128), F32)
    six = [padded(ref, 128) for ref in (v0, v1, v2, v3, v4, v5)]
    six = jnp.concatenate([*six, blank_row, blank_row], axis=0)
    six = pltpu.roll(six, lax.rem(device, 128 // part_rows) * part_rows, 1)
    lane_q = lax.rem(device * (3 * part_rows), 128)
    wide_q = jnp.concatenate([padded(bq_in, 256)] * 8, axis=0)
    wide_q = pltpu.roll(wide_q, lane_q, 1)
    vec[...] = jnp.concatenate(
        [six[0:6], wide_q[0:1, :128], wide_q[0:1, 128:], padded(bi_in, 128)]
        + [blank_row] * (SLOT - 9),
        axis=0,
    ).astype(BF)
    pos[...] = jnp.zeros_like(pos)
    pos[0:1, :] = padded(pos_in, pos.shape[1]).astype(jnp.int32)

    if neat:
        for n in range(3):
            for p in range(inner):
                at = (n * inner + p) * share
                pq[p, :, n * share : (n + 1) * share] = wq[:, at : at + share]
        piece_q = pq
    else:
        piece_q = wq
    swap_q = PlaneSwap(
        inner, g, r, lambda p: piece_q.at[p], lambda o: WQ.at[g, o], swap_s.at[0], swap_r.at[0]
    )
    swap_v = PlaneSwap(
        inner, g, r, lambda p: vec, lambda o: VEC.at[g, o], swap_s.at[1], swap_r.at[1]
    )
    swap_p = PlaneSwap(
        inner, g, r, lambda p: pos, lambda o: POS.at[o], swap_s.at[2], swap_r.at[2]
    )
    swap_v.start()
    swap_q.start()
    col_d = ColumnGather(outer, g, r, wd, WDZ, col_s.at[0], col_r.at[0])
    col_q = ColumnGather(outer, g, r, WQ.at[g], WQ, col_s.at[1], col_r.at[1])
    col_v = ColumnGather(outer, g, r, VEC.at[g], VEC, col_s.at[2], col_r.at[2])
    col_o = ColumnGather(outer, g, r, wo, WO, col_s.at[3], col_r.at[3])
    col_i = ColumnGather(outer, g, r, WI.at[g], WI, col_s.at[4], col_r.at[4])
    col_d.start()

    def slot(array, owner):
        return array.at[pl.ds(pl.multiple_of(owner * tok_rows, 16), tok_rows)]

    def tok(i, src, dst, to):
        return remote(src, dst, tok_s.at[i], tok_r.at[i], g, to)

    first_out = [
        tok(0, x, slot(X, r), by_a), tok(1, cot, slot(C, r), by_b),
        tok(2, cot, slot(C, r), by_a), tok(3, x, slot(X, r), by_b),
    ]
    for copy in first_out:
        copy.start()
    pair = [tok(6, x, slot(X, r), twin), tok(7, cot, slot(C, r), twin)]
    for copy in pair:
        copy.start()
    swap_p.start()
    own = [
        (x, slot(X, r)), (cot, slot(C, r)), (piece_q.at[r], WQ.at[g, r]), (vec, VEC.at[g, r]),
        (pos, POS.at[r]), (wd, WDZ.at[g]), (wo, WO.at[g]),
    ]
    own = [pltpu.make_async_copy(a, b, loc.at[i]) for i, (a, b) in enumerate(own)]
    for copy in own:
        copy.start()
    for copy in own:
        copy.wait()
    swap_v.arrive()
    col_v.start()
    swap_q.arrive()
    col_q.start()
    if neat:
        for n in range(outer):
            for p in range(inner):
                at = (n * inner + p) * 128
                pi[p, :, n * 128 : (n + 1) * 128] = wi[:, at : at + 128]
        piece_i = pi
    else:
        piece_i = wi
    swap_i = PlaneSwap(
        inner, g, r, lambda p: piece_i.at[p], lambda o: WI.at[g, o], swap_s.at[3], swap_r.at[3]
    )
    mine_i = pltpu.make_async_copy(piece_i.at[r], WI.at[g, r], loc.at[7])
    mine_i.start()

    def pass_on(index, array, owner):
        copy = tok(index, slot(array, owner), slot(array, owner), twin)
        copy.start()
        pair.append(copy)

    def landed(index, array, owner):
        tok(index, slot(array, owner), slot(array, owner), twin).wait_recv()

    col_d.forward()
    col_v.forward()
    col_v.arrive()
    lines = width // 128
    shift = lines.bit_length() - 1
    kinds = 6 * lines
    want = (kinds + 3 + 7) // 8 * 8
    o = lax.broadcasted_iota(jnp.int32, (want, count * SLOT), 0)
    c = lax.broadcasted_iota(jnp.int32, (want, count * SLOT), 1)
    d, n = c >> 4, c & 15
    line = (d * part_rows) >> 7
    plain = (o < kinds) & (n == (o >> shift)) & (line == (o & (lines - 1)))
    line_q = (d * (3 * part_rows)) >> 7
    goal = (o - kinds) * lines + r
    third = (o >= kinds) & (o < kinds + 3)
    third = third & (((n == 6) & (line_q == goal)) | ((n == 7) & (line_q + 1 == goal)))
    pick = jnp.where(plain | third, 1.0, 0.0).astype(BF)
    found = dot(pick, VEC[...].reshape(count * SLOT, 128), NN)

    def vector(k):
        return jnp.concatenate(
            [found[k * lines + j : k * lines + j + 1, :] for j in range(lines)], axis=1
        )

    for k in range(4):
        vecs[k : k + 1, :] = vector(k)
    vecs[4:5, :] = vector(4) + vector(5)
    bq[0:1, :] = jnp.concatenate([found[kinds + t : kinds + t + 1, :] for t in range(3)], axis=1)
    unit = hidden // outer
    bi[0:1, :] = jnp.concatenate(
        [VEC[z, r][8:9, :unit].astype(F32) for z in range(outer)], axis=1
    )

    def prepare(owner):
        at = pl.ds(pl.multiple_of(owner * tok_rows, 16), tok_rows)
        normed, _ = norm_stats(X[at, :])
        la[at, :] = (normed * vecs[0:1, :] + vecs[1:2, :]).astype(BF)
        LM[at, :] = (normed * vecs[2:3, :] + vecs[3:4, :]).astype(BF)

    landed(0, X, by_a)
    onward_a = tok(4, slot(X, by_a), slot(X, by_a), by_b)
    onward_a.start()
    pass_on(8, X, by_a)
    landed(1, C, by_b)
    onward_b = tok(5, slot(C, by_b), slot(C, by_b), by_a)
    onward_b.start()
    pass_on(9, C, by_b)
    swap_i.start()
    prepare(r)
    landed(6, X, twin)
    prepare(twin)
    col_d.arrive()
    for z in range(outer):
        owner = z * inner + r
        to, at = owner // outer, lax.rem(owner, outer)

        @pl.when(to == r)
        def _():
            WD[at] = WDZ[z]

        @pl.when(to != r)
        def _():
            remote(WDZ.at[z], WD.at[at], wd_s.at[z], wd_r.at[at], g, to).start()

    prepare(by_a)
    landed(2, C, by_a)
    pass_on(10, C, by_a)
    landed(3, X, by_b)
    pass_on(11, X, by_b)
    col_q.forward()
    col_o.start()
    prepare(by_b)
    landed(8, X, twin ^ 2)
    prepare(twin ^ 2)
    swap_p.arrive()
    lane_parts = []
    for p in range(inner):
        lane_parts.append(POS[p].astype(F32)[0:1, :tok_rows])
    place[0:1, :] = jnp.concatenate(lane_parts, axis=1)
    step_of = lax.broadcasted_iota(jnp.int32, (half, rows), 0).astype(F32)
    angles = place[0:1, :] * jnp.exp(step_of * (-2.0 / ROT * jnp.log(ROPE_BASE)))
    cos_t, sin_t = jnp.cos(angles), jnp.sin(angles)
    blank = jnp.zeros((half, rows), F32)
    quiet = jnp.zeros((HD - ROT, rows), F32)
    tall = lambda parts: jnp.transpose(jnp.concatenate(parts * heads, axis=0))
    cosine[...] = tall([cos_t, cos_t, quiet + 1.0])
    lower[...] = tall([-sin_t, blank, quiet])
    upper[...] = tall([blank, sin_t, quiet])
    landed(4, X, diag)
    pass_on(12, X, diag)
    landed(5, C, diag)
    pass_on(13, C, diag)
    landed(11, X, twin ^ 4)
    prepare(twin ^ 4)
    prepare(diag)
    landed(12, X, twin ^ 6)
    prepare(twin ^ 6)
    for i, owner in ((7, twin), (9, twin ^ 4), (10, twin ^ 2), (13, twin ^ 6)):
        landed(i, C, owner)
    for z in range(outer):
        source = lax.rem(r * outer + z, inner)

        @pl.when(source != r)
        def _():
            remote(WD.at[z], WD.at[z], wd_s.at[z], wd_r.at[z], g, source).wait_recv()

    col_q.arrive()
    mine_i.wait()
    swap_i.arrive()
    col_i.start()

    def turn(values, at, orient):
        ahead_v = pltpu.roll(values, share - half, 1)
        behind_v = pltpu.roll(values, half, 1)
        return values * cosine[at, :] + orient * (ahead_v * lower[at, :] + behind_v * upper[at, :])

    def chunk(i):
        return pl.ds(pl.multiple_of(i * block, block), block)

    def ahead(i):
        return pl.ds(pl.multiple_of(i * block + REACH, block), block)

    w_qkv = lambda: WQ[...].reshape(width, 3 * share)
    w_dense = lambda: WD[...].reshape(share, width)

    def project(j, carry):
        i = chunks - 1 - j
        at = chunk(i)
        mixed = dot(la[at, :], w_qkv(), NN) + bq[0:1, :]
        q[at, :] = turn(mixed[:, :share], at, 1.0).astype(BF)
        kk[ahead(i), :] = turn(mixed[:, share : 2 * share], at, 1.0).astype(BF)
        vv[ahead(i), :] = mixed[:, 2 * share :].astype(BF)
        gc[at, :] = dot(C[at, :], w_dense(), NT).astype(BF)
        return carry

    first, last = pl.ds(0, REACH), pl.ds(rows, REACH)

    def halo(n, src, dst, to):
        return remote(src, dst, halo_s.at[n], halo_r.at[n], to, r)

    lax.fori_loop(0, tail, project, 0)

    @pl.when(g < outer - 1)
    def _():
        halo(0, kk.at[last], kk.at[first], g + 1).start()
        halo(1, vv.at[last], vv.at[first], g + 1).start()

    @pl.when(g == 0)
    def _():
        kk[first, :] = jnp.zeros((REACH, share), BF)
        vv[first, :] = jnp.zeros((REACH, share), BF)

    lax.fori_loop(tail, chunks, project, 0)
    gk[...] = jnp.zeros_like(gk)
    gv[...] = jnp.zeros_like(gv)

    def attend(i, carry):
        at = chunk(i)
        keys = pl.ds(pl.multiple_of(i * block, block), span)
        reach = place[0:1, at].astype(jnp.int32)
        spread = (
            lax.broadcasted_iota(jnp.int32, (span, block), 1) + REACH
            - lax.broadcasted_iota(jnp.int32, (span, block), 0)
        )
        allowed = (spread >= 0) & (spread <= reach)
        ctx_h, gq_h, gk_h, gv_h = [], [], [], []
        for h in range(heads):
            lanes = slice(h * HD, (h + 1) * HD)
            q_h, gc_h = q[at, lanes], gc[at, lanes]
            k_h, v_h = kk[keys, lanes], vv[keys, lanes]
            scores = jnp.where(allowed, dot(k_h, q_h, NT) * HD ** (-0.5), -1e30)
            top = jnp.max(scores, axis=0, keepdims=True)
            weight = jnp.exp(scores - top)
            probs = weight * (1.0 / jnp.sum(weight, axis=0, keepdims=True))
            probs_b = probs.astype(BF)
            ctx_h.append(dot(probs_b, v_h, TN))
            grad_probs = dot(v_h, gc_h, NT)
            row_dot = jnp.sum(probs * grad_probs, axis=0, keepdims=True)
            grad_s = (probs * (grad_probs - row_dot) * HD ** (-0.5)).astype(BF)
            gq_h.append(dot(grad_s, k_h, TN))
            gk_h.append(dot(grad_s, q_h, NN))
            gv_h.append(dot(probs_b, gc_h, NN))
        ctx[at, :] = jnp.concatenate(ctx_h, axis=1).astype(BF)
        gq[at, :] = jnp.concatenate(gq_h, axis=1)
        gk[keys, :] += jnp.concatenate(gk_h, axis=1)
        gv[keys, :] += jnp.concatenate(gv_h, axis=1)
        return carry

    lax.fori_loop(tail, chunks, attend, 0)
    col_o.forward()

    @pl.when(g > 0)
    def _():
        halo(0, kk.at[first], kk.at[first], g).wait_recv()
        halo(1, vv.at[first], vv.at[first], g).wait_recv()

    lax.fori_loop(0, tail, attend, 0)
    away[0] = gk[first, :].astype(BF)
    away[1] = gv[first, :].astype(BF)

    @pl.when(g > 0)
    def _():
        halo(2, away, back, g - 1).start()

    @pl.when(g == outer - 1)
    def _():
        back[...] = jnp.zeros_like(back)

    table[...] = jnp.zeros_like(table)

    def finish(i, carry):
        at = chunk(i)
        grads = jnp.concatenate(
            [
                turn(gq[at, :], at, -1.0), turn(gk[ahead(i), :], at, -1.0),
                gv[ahead(i), :],
            ],
            axis=1,
        )
        table[5:6, : 3 * share] += column_sum(grads)
        grads_b = grads.astype(BF)
        gb[at, :] = grads_b
        grad_left = dot(grads_b, w_qkv(), NT)
        normed, _ = norm_stats(X[at, :])
        table[0:1, :] += column_sum(grad_left * normed)
        table[1:2, :] += column_sum(grad_left)
        GN[at, :] = (grad_left * vecs[0:1, :]).astype(BF)
        return carry

    lax.fori_loop(0, chunks - tail, finish, 0)
    col_i.forward()

    @pl.when(g < outer - 1)
    def _():
        halo(2, away, back, g).wait_recv()

    gk[last, :] += back[0].astype(F32)
    gv[last, :] += back[1].astype(F32)
    lax.fori_loop(chunks - tail, chunks, finish, 0)

    sum_q = ColumnSum(outer, g, r, gq_w, gq_l, sum_s.at[0], sum_r.at[0])
    sum_i = ColumnSum(outer, g, r, gi_w, gi_l, sum_s.at[1], sum_r.at[1])
    sum_o = ColumnSum(outer, g, r, go_w, go_l, sum_s.at[2], sum_r.at[2])
    sum_d = ColumnSum(outer, g, r, gd_z, gd_l, sum_s.at[3], sum_r.at[3])
    part = inner * part_rows
    for t in range(outer):
        grad = dot(la[:, t * part : (t + 1) * part], gb[...], TN).astype(BF)
        gq_w[t] = grad.reshape(gq_w.shape[1:])
    sum_q.start()
    lanes_d = min(width, 256)
    for t in range(width // lanes_d):
        at = slice(t * lanes_d, (t + 1) * lanes_d)
        grad = dot(ctx[...], C[:, at], TN).astype(BF)
        gd_w[:, :, at] = grad.reshape(outer, part_rows, lanes_d)
    for i in range(outer):
        owner = r * outer + i
        z, to = owner // inner, lax.rem(owner, inner)

        @pl.when(to == r)
        def _():
            gd_z[z] = gd_w[i]

        @pl.when(to != r)
        def _():
            remote(gd_w.at[i], gd_z.at[z], gd_ss.at[i], gd_rs.at[z], g, to).start()

    col_o.arrive()
    col_i.arrive()
    w_in = lambda: WI[...].reshape(width, hidden)
    w_out = lambda: WO[...].reshape(hidden, width)

    def inside(i, carry):
        at = chunk(i)
        pre_act = dot(LM[at, :], w_in(), NN) + bi[0:1, :]
        activated, slope = gelu_pair(pre_act)
        act[at, :] = activated.astype(BF)
        grad_pre = dot(C[at, :], w_out(), NT) * slope
        gp[at, :] = grad_pre.astype(BF)
        table[6:7, :hidden] += column_sum(grad_pre)
        return carry

    sum_q.rest()
    lax.fori_loop(0, chunks, inside, 0)
    for t in range(outer):
        go_w[t] = dot(act[:, t * unit : (t + 1) * unit], C[...], TN).astype(BF)
    sum_o.start()
    for t in range(outer):
        grad = dot(LM[:, t * part : (t + 1) * part], gp[...], TN).astype(BF)
        gi_w[t] = grad.reshape(gi_w.shape[1:])
    sum_i.start()
    for z in range(outer):
        source = (z * inner + r) // outer

        @pl.when(source != r)
        def _():
            remote(gd_z.at[z], gd_z.at[z], gd_ss.at[z], gd_rs.at[z], g, source).wait_recv()

    sum_d.start()
    sum_d.rest()
    sum_q.middle()

    def outside(i, carry):
        at = pl.ds(pl.multiple_of(i * tok_rows, 16), tok_rows)
        mlp_out = dot(act[at, :], w_out(), NN)
        out_p[i] = (dot(ctx[at, :], w_dense(), NN) + mlp_out).astype(BF)
        grad_left = dot(gp[at, :], w_in(), NT)
        normed, _ = norm_stats(X[at, :])
        table[2:3, :] += column_sum(grad_left * normed)
        table[3:4, :] += column_sum(grad_left)
        gn_p[i] = (GN[at, :].astype(F32) + grad_left * vecs[2:3, :]).astype(BF)
        return carry

    lax.fori_loop(0, inner // 2, outside, 0)
    sum_o.rest()
    sum_i.rest()
    lax.fori_loop(inner // 2, inner, outside, 0)
    plane_o = PlaneSum(inner, g, r, out_p, out_b, out_m, out_l, pl_s.at[0], pl_r.at[0])
    plane_n = PlaneSum(inner, g, r, gn_p, gn_b, gn_m, gn_l, pl_s.at[1], pl_r.at[1])
    plane_n.start()
    plane_o.start()
    top_f = cot[...].astype(F32)
    table[4:5, :] = column_sum(top_f)
    col_t = ColumnGather(outer, g, r, table, table_z, col_s.at[5], col_r.at[5])
    col_t.start()
    sum_o.middle()
    sum_i.middle()
    plane_n.middle()
    plane_o.middle()
    sum_d.middle()
    col_t.forward()
    sum_q.total(gq_t)
    gq_s[...] = gq_t[...].astype(BF)
    swap_gq = PlaneSwap(
        inner, g, r, lambda p: gq_s.at[p], lambda o: gq_e.at[o], swap_s.at[4], swap_r.at[4]
    )
    swap_gq.start()
    gq_e[r] = gq_s[r]
    col_t.arrive()
    table_z[g] = table[...]
    TS[r] = jnp.sum(table_z[...], axis=0)
    swap_t = PlaneSwap(
        inner, g, r, lambda p: TS.at[r], lambda o: TS.at[o], swap_s.at[5], swap_r.at[5]
    )
    swap_t.start()
    plane_o.total(total)
    x_f = x[...].astype(F32)
    RES[...] = (x_f + total[...] + vecs[4:5, :]).astype(BF)
    plane_n.total(total)
    own_normed, inv_scale = norm_stats(x[...])
    grad_normed = total[...]
    GIN[...] = top_f + inv_scale * (
        grad_normed
        - jnp.mean(grad_normed, axis=-1, keepdims=True)
        - own_normed * jnp.mean(grad_normed * own_normed, axis=-1, keepdims=True)
    )
    sum_o.total(go_f)
    sum_d.total(gd_f)
    sum_i.total(gi_t)
    gi_s[...] = gi_t[...].astype(BF)
    swap_gi = PlaneSwap(
        inner, g, r, lambda p: gi_s.at[p], lambda o: gi_e.at[o], swap_s.at[6], swap_r.at[6]
    )
    swap_gi.start()
    gi_e[r] = gi_s[r]

    def settle(out, arrived):
        if not neat:
            out[...] = arrived[...]
            return
        for owner in range(inner):
            for n in range(arrived.shape[2] // 128):
                at = (n * inner + owner) * 128
                out[:, at : at + 128] = arrived[owner][:, n * 128 : n * 128 + 128].astype(F32)

    swap_gq.arrive()
    settle(GQ, gq_e)
    swap_t.arrive()
    TSUM[...] = jnp.sum(TS[...], axis=0)
    swap_gi.arrive()
    settle(GI, gi_e)
    for copy in first_out + pair + [onward_a, onward_b]:
        copy.wait_send()
    for i in range(outer):
        to = (i * inner + r) // outer

        @pl.when(to != r)
        def _():
            remote(WDZ.at[i], WD.at[i], wd_s.at[i], wd_r.at[i], g, to).wait_send()

        to = lax.rem(r * outer + i, inner)

        @pl.when(to != r)
        def _():
            remote(gd_w.at[i], gd_z.at[i], gd_ss.at[i], gd_rs.at[i], g, to).wait_send()

    @pl.when(g < outer - 1)
    def _():
        halo(0, kk.at[last], kk.at[first], g).wait_send()
        halo(1, vv.at[last], vv.at[first], g).wait_send()

    @pl.when(g > 0)
    def _():
        halo(2, away, back, g).wait_send()

    for item in (
        swap_q, swap_v, swap_p, swap_i, col_d, col_q, col_v, col_o, col_i, plane_o, plane_n,
        sum_q, sum_i, sum_o, sum_d, col_t, swap_gq, swap_gi, swap_t,
    ):
        item.sent()


def layer(outer, inner, x, cot, pos, vectors, wq, wi, wd, wo):
    shape = jax.ShapeDtypeStruct
    dma = pltpu.SemaphoreType.DMA
    vmem = pl.BlockSpec(memory_space=pltpu.VMEM)
    tok_rows, width = x.shape
    part_rows, unit = wd.shape[0], wo.shape[0]
    rows = inner * tok_rows
    share = width // inner
    hidden = outer * unit
    lanes = -(-tok_rows // 128) * 128
    neat = whole_tiles(unit, share, part_rows)
    chips = inner // 2
    v = pltpu.VMEM
    piece_q = (inner, part_rows, 3 * share)
    piece_i = (inner, part_rows, hidden)
    piece_o = (unit, width)
    piece_d = (part_rows, width)
    outs = (
        shape((tok_rows, width), BF), shape((tok_rows, width), F32),
        shape((part_rows, 3 * width), F32) if neat else shape(piece_q, BF),
        shape((part_rows, hidden * inner), F32) if neat else shape(piece_i, BF),
        shape(piece_o, F32), shape(piece_d, F32), shape((inner, 8, width), F32),
        shape((8, width), F32),
    )
    wide = v((rows, width), BF)
    own = (rows, share)
    more = (rows + REACH, share)
    quad = v((chips, tok_rows, width), BF)
    group = v((inner, tok_rows, width), BF)
    scratch = [
        wide, wide, v((inner, 8, lanes), jnp.int32), v((outer, inner, SLOT, 128), BF),
        v((outer, *piece_q), BF), v((outer, *piece_d), BF), v((outer, *piece_d), BF),
        v((outer, *piece_i), BF), v((outer, *piece_o), BF), v(piece_q, BF), v(piece_i, BF),
        v((8, width), F32), v((8, 3 * share), F32), v((8, hidden), F32), v((8, rows), F32),
        wide, wide, wide, v((outer, *piece_q), BF), v((outer, *piece_d), BF),
        v(own, BF), v(own, BF), v(more, BF), v(more, BF), v(own, F32), v(more, F32),
        v(more, F32), v(own, BF), v((rows, 3 * share), BF), v(own, F32), v(own, F32),
        v(own, F32), v((2, REACH, share), BF), v((2, REACH, share), BF),
        v((rows, hidden), BF), v((rows, hidden), BF), group, group, *([quad] * 6),
        v((outer, *piece_i), BF), v((outer, *piece_o), BF),
        v((outer + 1, *piece_i), BF), v((outer + 1, *piece_o), BF),
        v((outer + 1, *piece_q), BF), v((outer + 1, *piece_d), BF), v((outer, *piece_d), BF),
        v(piece_q, F32), v(piece_i, F32), v(piece_q, BF), v(piece_i, BF),
        v(piece_q, BF), v(piece_i, BF), v((8, width), F32), v((outer, 8, width), F32),
        v((tok_rows, width), F32), v((SLOT, 128), BF), v((8, lanes), jnp.int32),
        dma((8,)), dma((14,)), dma((14,)), dma((7, inner)), dma((7, inner)),
        dma((6, outer + 1)), dma((6, outer + 1)), dma((outer,)), dma((outer,)),
        dma((3,)), dma((3,)), dma((2, 2 * chips)), dma((2, 2 * chips)),
        dma((4, outer + 1)), dma((4, outer + 1)), dma((outer,)), dma((outer,)),
    ]
    out = pl.pallas_call(
        functools.partial(layer_kernel, outer, inner, neat),
        out_shape=outs,
        in_specs=[vmem] * 15,
        out_specs=[vmem] * 8,
        scratch_shapes=scratch,
        compiler_params=pltpu.CompilerParams(
            collective_id=0, has_side_effects=True, vmem_limit_bytes=VMEM_LIMIT
        ),
    )(x, cot, pos, *vectors, wq, wi, wd, wo)
    out = deliver(outer, inner, part_rows, unit, share, out)
    if not neat:
        for n, parts in ((2, 3), (3, outer)):
            out[n] = (
                out[n].reshape(inner, part_rows, parts, -1)
                .transpose(1, 2, 0, 3)
                .reshape(part_rows, -1)
                .astype(F32)
            )
    return out


def deliver_kernel(outer, inner, part_rows, unit, share, *refs):
    big, (TS, TSUM), outs = refs[:6], refs[6:8], refs[8:]
    copied, small, (spread, sems) = outs[:6], outs[6:14], outs[14:]
    copies = [
        pltpu.make_async_copy(a, b, sems.at[i]) for i, (a, b) in enumerate(zip(big, copied))
    ]
    for copy in copies:
        copy.start()
    g, r = lax.axis_index("g"), lax.axis_index("r")
    device = g * inner + r
    width = TSUM.shape[1]
    sums = pltpu.roll(TSUM[...], lax.rem(width - device * part_rows, width), 1)
    for out, n in zip(small[:6], (0, 1, 2, 3, 4, 4)):
        out[...] = sums[n : n + 1, :part_rows]
    spread[...] = jnp.zeros_like(spread)
    for t in range(3):
        for p in range(inner):
            row = t * inner + p
            spread[row : row + 1, :] = TS[p][5:6, t * share : (t + 1) * share]
    size = 3 * part_rows
    row, lane = (device * size) // 128, lax.rem(device * size, 128)
    two = jnp.concatenate([spread[pl.ds(row, 1), :], spread[pl.ds(row + 1, 1), :]], axis=1)
    two = pltpu.roll(jnp.concatenate([two] * 8, axis=0), lax.rem(256 - lane, 256), 1)
    small[6][...] = two[0:1, :size]
    mine = pltpu.roll(TS[r], lax.rem(width - g * unit, width), 1)
    small[7][...] = mine[6:7, :unit]
    for copy in copies:
        copy.wait()


def deliver(outer, inner, part_rows, unit, share, arrays):
    shape = jax.ShapeDtypeStruct
    vmem = pl.BlockSpec(memory_space=pltpu.VMEM)
    any_spec = pl.BlockSpec(memory_space=pl.ANY)
    sizes = [part_rows] * 6 + [3 * part_rows, unit]
    out = pl.pallas_call(
        functools.partial(deliver_kernel, outer, inner, part_rows, unit, share),
        out_shape=[shape(a.shape, a.dtype) for a in arrays[:6]]
        + [shape((1, n), F32) for n in sizes],
        in_specs=[vmem] * 8,
        out_specs=[any_spec] * 6 + [vmem] * 8,
        scratch_shapes=[
            pltpu.VMEM((3 * inner + 8, 128), F32), pltpu.SemaphoreType.DMA((6,)),
        ],
    )(*arrays)
    return list(out[:6]) + [a.reshape(-1) for a in out[6:]]


def whole_tiles(unit, share, part_rows):
    return unit == 128 and share == 128 and part_rows % 16 == 0


def body(
    layer_input,
    ln1_gain,
    ln1_bias,
    qkv_weight,
    qkv_bias,
    dense_weight,
    dense_bias,
    ln2_gain,
    ln2_bias,
    fc_in_weight,
    fc_in_bias,
    fc_out_weight,
    fc_out_bias,
    positions,
    cotangent,
):
    bf = jnp.bfloat16
    f32 = jnp.float32
    outer = lax.axis_size("g")
    inner = lax.axis_size("r")
    count = outer * inner
    rank = lax.axis_index("r")
    tok_rows, width = layer_input.shape
    part_rows = qkv_weight.shape[0]
    share = width // inner
    unit = fc_out_weight.shape[0]
    hidden = outer * unit
    rows = inner * tok_rows

    vectors = [
        ln1_gain, ln1_bias, ln2_gain, ln2_bias, dense_bias, fc_out_bias, qkv_bias, fc_in_bias
    ]
    vectors = [v[None] for v in vectors]
    wq, wi = qkv_weight, fc_in_weight
    if not whole_tiles(unit, share, part_rows):
        wq = (
            wq.reshape(part_rows, 3, inner, share)
            .transpose(2, 0, 1, 3)
            .reshape(inner, part_rows, 3 * share)
        )
        wi = (
            wi.reshape(part_rows, outer, inner, unit)
            .transpose(2, 0, 1, 3)
            .reshape(inner, part_rows, hidden)
        )
    out = layer(
        outer, inner, layer_input, cotangent, positions[None], vectors, wq, wi,
        dense_weight, fc_out_weight,
    )
    result, grad_in, g_qkv_w, g_in_w, g_out_w, g_dense_w = out[:6]
    g_gain1, g_shift1, g_gain2, g_shift2, g_dense_b, g_out_b, g_qkv_b, g_in_b = out[6:]
    return (
        result,
        grad_in,
        g_gain1,
        g_shift1,
        g_qkv_w,
        g_qkv_b,
        g_dense_w,
        g_dense_b,
        g_gain2,
        g_shift2,
        g_in_w,
        g_in_b,
        g_out_w,
        g_out_b,
    )


def solution(mesh):
    inner = GROUP
    split = Mesh(mesh.devices.reshape(-1, inner), ("g", "r"))
    flat = P(("g", "r"))
    tall = P(("g", "r"), None)
    in_specs = (
        tall, flat, flat, tall, flat, tall, flat, flat, flat, tall, flat, tall, flat, flat, tall,
    )
    out_specs = (
        tall, tall, flat, flat, tall, flat, tall, flat, flat, flat, tall, flat, tall, flat,
    )
    return jax.shard_map(body, mesh=split, in_specs=in_specs, out_specs=out_specs, check_vma=False)
```
